32 devices in a mesh: rep: 4 (over y, x), shard: 2 (over core), exp: 4 (over z).
Axes of the slice: x: 2, y: 2, z: 4, core: 2. Of those that a mesh axis runs over, the one named last changes fastest.
Arguments:
- tokens: bfloat16 [2048, 2560], P(('rep', 'exp')), may hold values from -6 to 6
- expert_of: int32 [2048, 1], P(('rep', 'exp')), may hold values from 0 to 3; in each aligned block of 128 rows (0 to 127, 128 to 255, ...) at most 80 rows name the same one
- w_gate: bfloat16 [4, 768, 2560], P('exp', 'shard'), may hold values from -0.125 to 0.125
- w_up: bfloat16 [4, 768, 2560], P('exp', 'shard'), may hold values from -0.125 to 0.125
- d_hidden: bfloat16 [4, 4, 4, 80, 768], P('rep', 'exp', None, None, 'shard'), may hold values from -6 to 6
Outputs:
- hidden: bfloat16 [4, 4, 4, 80, 768], P('rep', 'exp', None, None, 'shard')
- d_tokens: bfloat16 [2048, 2560], P(('rep', 'exp'), 'shard')
- grad_gate: bfloat16 [4, 768, 2560], P('exp', 'shard')
- grad_up: bfloat16 [4, 768, 2560], P('exp', 'shard')
The draws below stay inside these ranges and needn't reach their ends.
Inputs may be any that keep to these rules, and one draw needn't show every extreme that they name: `expert_of`: each value names an expert. Among the 128 tokens of one device (aligned blocks of rows), no expert is named more than 80 times, a bound that some block reaches.
All inputs are finite; a program needn't handle non-finite values.
Results may differ from the reference program's by a relative error of at most 0.017.
Values may be sent and summed in bfloat16 or wider, within the bound.
No kernel may reach another device: no remote copies, remote signals or barrier semaphores. Data moves between devices by JAX's collectives and lax.ppermute only.
A program may use at most 64 MiB of HBM per device.

```python
import math
import jax
import jax.numpy as jnp
import numpy as np
from jax import lax

D = 2560
FF = 768
TOK_DEV = 128
EXPERTS = 4
CAP = 80
TOKENS = 2048
N_REP = 4
N_SHARD = 2
N_EXP = 4


def steps_of(own_key, extent, cuts, low, high):
    loudness = 1.0
    for dim, parts in cuts:
        heights = jax.random.uniform(jax.random.fold_in(jax.random.fold_in(own_key, 6), dim), (parts,), jnp.float32, low / len(cuts), high / len(cuts))
        loudness = loudness * jnp.repeat(jnp.exp(heights), extent[dim] // parts).reshape((-1,) + (1,) * (len(extent) - 1 - dim))
    return loudness


def shared_out(rng, own, number, rows, amount, top, limit, skew):
    order = jax.random.permutation(rng, amount)
    crowded, common = shares(amount, rows * top, limit, skew, True), shares(amount, rows * top, limit, skew, False)
    places = jnp.arange(amount)

    def named(lengths, rotation):
        used = int((lengths > 0).sum())
        fixed = max(1, used // 4)
        passed = fixed + (places - fixed + rotation * (used - fixed)) % max(1, amount - fixed)
        return jnp.zeros((amount,), jnp.int32).at[order[jnp.where(places < fixed, places, passed)]].set(jnp.asarray(lengths, jnp.int32))

    lengths = jnp.where(number % 4 == 0, named(crowded, number // 4), named(common, number - number // 4 - 1))
    mixed = jax.random.permutation(jax.random.fold_in(own, 3), amount)
    giver, receiver = mixed[0:amount // 2 * 2:2], mixed[1:amount // 2 * 2:2]
    room = jnp.minimum(lengths[giver] - 1, limit - lengths[receiver]) // 2
    room = jnp.where((giver == order[0]) | (receiver == order[0]) | (lengths[receiver] == 0), 0, jnp.maximum(room, 0))
    passed = jax.random.randint(jax.random.fold_in(own, 4), (amount // 2,), 0, 1 << 20) % (room + 1)
    lengths = lengths.at[giver].add(-passed).at[receiver].add(passed)
    items = jnp.searchsorted(jnp.cumsum(lengths), jnp.arange(rows * top), side="right").astype(jnp.int32)
    table = items.reshape(top, rows).T
    table = table[jax.random.permutation(jax.random.fold_in(own, 1), rows)]
    rotation = jax.random.randint(jax.random.fold_in(own, 2), (rows, 1), 0, top)
    return jnp.take_along_axis(table, (jnp.arange(top)[None, :] + rotation) % top, axis=1)


def shares(amount, total, reach, skew, full):
    portions = [(1 << 20) // math.isqrt(rank ** skew) + 1 for rank in range(1, amount + 1)]
    largest = reach if full else min(reach, max(-(-total // amount), total * portions[0] // sum(portions)))
    least = 1 if total - largest >= amount - 1 else 0
    holding, spare = [largest] + [least] * (amount - 1), total - largest - least * (amount - 1)
    while spare > 0:
        candidates = [i for i in range(1, amount) if holding[i] < largest] or [i for i in range(1, amount) if holding[i] < reach]
        whole, left = sum([portions[i] for i in candidates]), spare
        for i in candidates:
            more = min(reach - holding[i], max(1, left * portions[i] // whole), spare)
            holding[i] = holding[i] + more
            spare = spare - more
    return np.array(holding)


def noise(key, dims, width, limit, shards=(), held_as=jnp.bfloat16):
    gain = steps_of(key, dims, shards, -0.22, 0.18) if shards else 1.0
    values = jax.random.normal(key, dims, jnp.float32) * width * gain
    return jnp.minimum(jnp.maximum(values, -limit), limit).astype(held_as)


def setup_inputs(seed: int = 0) -> dict:
    keys = jax.random.split(jax.random.key(seed), 6)
    tokens = noise(keys[0], (TOKENS, D), 1.0, 6.0, ((0, 16),))
    expert_of_keys = jax.random.split(jax.random.fold_in(keys[1], 1), TOKENS // TOK_DEV)
    expert_of_turns = jax.random.permutation(jax.random.fold_in(keys[1], 3), TOKENS // TOK_DEV)
    expert_of = jax.vmap(lambda own, number: shared_out(jax.random.fold_in(keys[1], 2), own, number, TOK_DEV, EXPERTS, 1, CAP, 2))(expert_of_keys, expert_of_turns).reshape((TOKENS, 1))
    w_gate = noise(keys[2], (EXPERTS, FF, D), D ** -0.5, 0.125, ((0, 4), (1, 2)))
    w_up = noise(keys[3], (EXPERTS, FF, D), D ** -0.5, 0.125, ((0, 4), (1, 2)))
    d_hidden = noise(keys[4], (N_REP, EXPERTS, N_EXP, CAP, FF), 1.0, 6.0, ((0, 4), (1, 4), (4, 2)))
    return dict(tokens=tokens, expert_of=expert_of, w_gate=w_gate, w_up=w_up, d_hidden=d_hidden)


def reference(tokens, expert_of, w_gate, w_up, d_hidden):
    feats = tokens.reshape(N_REP, N_EXP, TOK_DEV, D)
    routed = expert_of.reshape(N_REP, N_EXP, TOK_DEV)
    labels = jnp.arange(EXPERTS, dtype=jnp.int32)
    chosen = (routed[..., None] == labels).astype(jnp.int32)
    slot_index = jnp.sum(chosen * (jnp.cumsum(chosen, axis=2) - 1), axis=-1).astype(jnp.int32)
    source_index = jnp.broadcast_to(jnp.arange(N_EXP, dtype=jnp.int32)[:, None], (N_EXP, TOK_DEV))
    gate_full = w_gate.astype(jnp.float32)
    up_full = w_up.astype(jnp.float32)
    quarter = FF // N_SHARD
    total_gate = jnp.zeros((EXPERTS, FF, D), jnp.float32)
    total_up = jnp.zeros((EXPERTS, FF, D), jnp.float32)
    hidden_list = []
    grad_list = []
    for group in range(N_REP):
        buffer = jnp.zeros((EXPERTS, N_EXP, CAP, D), jnp.bfloat16)
        buffer = buffer.at[routed[group], source_index, slot_index[group]].set(feats[group])
        packed = buffer.astype(jnp.float32)
        gate_act = jnp.einsum('ejcd,efd->ejcf', packed, gate_full)
        up_act = jnp.einsum('ejcd,efd->ejcf', packed, up_full)
        sigma = jax.nn.sigmoid(gate_act)
        hidden_list.append((gate_act * sigma * up_act).astype(jnp.bfloat16))
        cotan = d_hidden[group].astype(jnp.float32)
        grad_gate_act = (cotan * up_act * sigma * (1.0 + gate_act * (1.0 - sigma))).astype(jnp.bfloat16).astype(jnp.float32)
        grad_up_act = (cotan * gate_act * sigma).astype(jnp.bfloat16).astype(jnp.float32)
        part_gate = jnp.einsum('ejcf,ejcd->efd', grad_gate_act, packed)
        part_up = jnp.einsum('ejcf,ejcd->efd', grad_up_act, packed)
        total_gate = total_gate + lax.optimization_barrier(part_gate.astype(jnp.bfloat16)).astype(jnp.float32)
        total_up = total_up + lax.optimization_barrier(part_up.astype(jnp.bfloat16)).astype(jnp.float32)
        summed = jnp.zeros((EXPERTS, N_EXP, CAP, D), jnp.float32)
        for piece in range(N_SHARD):
            lower = piece * quarter
            upper = lower + quarter
            term = jnp.einsum('ejcf,efd->ejcd', grad_gate_act[..., lower:upper], gate_full[:, lower:upper, :])
            term = term + jnp.einsum('ejcf,efd->ejcd', grad_up_act[..., lower:upper], up_full[:, lower:upper, :])
            summed = summed + lax.optimization_barrier(term.astype(jnp.bfloat16)).astype(jnp.float32)
        d_packed = summed.astype(jnp.bfloat16)
        grad_list.append(d_packed[routed[group], source_index, slot_index[group]])
    hidden = jnp.stack(hidden_list)
    d_tokens = jnp.stack(grad_list).reshape(TOKENS, D)
    grad_gate = (total_gate * (1.0 / N_REP)).astype(jnp.bfloat16)
    grad_up = (total_up * (1.0 / N_REP)).astype(jnp.bfloat16)
    return (hidden, d_tokens, grad_gate, grad_up)
```

```python
import jax
import jax.numpy as jnp
from jax import lax
from jax.sharding import PartitionSpec as P

BF16 = jnp.bfloat16
F32 = jnp.float32
LAST = (((1,), (1,)), ((), ()))
FIRST = (((0,), (0,)), ((), ()))
MATMUL = (((1,), (0,)), ((), ()))


def dot(a, b, dims):
    return lax.dot_general(a, b, dims, preferred_element_type=F32)


def targets(expert_of, expert_count, capacity, first):
    routed = expert_of[:, 0]
    chosen = (routed[:, None] == jnp.arange(expert_count, dtype=jnp.int32)[None, :]).astype(
        jnp.int32
    )
    slot_index = jnp.sum(chosen * (jnp.cumsum(chosen, axis=0) - 1), axis=1)
    return lax.rem(routed - first + expert_count, expert_count) * capacity + slot_index


def placement(target, slots_all):
    return (jnp.arange(slots_all, dtype=jnp.int32)[:, None] == target[None, :]).astype(BF16)


def gradients(gate_act, up_act, cotan):
    sigma = jax.nn.sigmoid(gate_act)
    cotan = cotan.astype(F32)
    d_gate = (cotan * up_act * sigma * (1.0 + gate_act * (1.0 - sigma))).astype(BF16)
    d_up = (cotan * gate_act * sigma).astype(BF16)
    return sigma, d_gate, d_up


def reduce_plan(tokens, expert_of, w_gate, w_up, d_hidden):
    expert_count = lax.axis_size("exp")
    replica_count = lax.axis_size("rep")
    capacity = d_hidden.shape[3]
    feature_width = tokens.shape[1]
    slots_all = expert_count * capacity
    placing = placement(targets(expert_of, expert_count, capacity, 0), slots_all)
    packed = dot(placing, tokens, MATMUL).astype(BF16)
    arrived = lax.all_to_all(
        packed.reshape(expert_count, capacity, feature_width), "exp", 0, 0, tiled=True
    )
    rows = arrived.reshape(slots_all, feature_width)
    gate_act, up_act = dot(rows, w_gate[0], LAST), dot(rows, w_up[0], LAST)
    cotan = d_hidden.reshape(slots_all, w_gate.shape[1])
    sigma, d_gate, d_up = gradients(gate_act, up_act, cotan)
    hidden = (gate_act * sigma * up_act).astype(BF16)

    def reduced(d_act):
        total = lax.psum(dot(d_act, rows, FIRST).astype(BF16), "rep").astype(F32)
        return (total * (1.0 / replica_count)).astype(BF16)[None]

    term = dot(d_gate, w_gate[0], MATMUL) + dot(d_up, w_up[0], MATMUL)
    outgoing = term.astype(BF16).reshape(expert_count, capacity, feature_width)
    returned = lax.all_to_all(outgoing, "exp", 0, 0, tiled=True)
    unpacked = dot(placing, returned.reshape(slots_all, feature_width), FIRST)
    d_tokens = lax.psum_scatter(unpacked.astype(BF16), "shard", scatter_dimension=1, tiled=True)
    return hidden.reshape(d_hidden.shape), d_tokens, reduced(d_gate), reduced(d_up)


def across(x, axis, bit):
    size = lax.axis_size(axis)
    return lax.ppermute(x, axis, [(i, i ^ bit) for i in range(size)])


def turned(x, axis, step):
    size = lax.axis_size(axis)
    return lax.ppermute(x, axis, [(i, (i + step) % size) for i in range(size)])


def gather_rep(x):
    half = x.shape[0] // 2
    a, b = x[:half], x[half:]
    a1, b2 = across(a, "rep", 1), across(b, "rep", 2)
    near = jnp.concatenate([a1, b2])
    a23 = across(jnp.concatenate([a, a1]), "rep", 2)
    b13 = across(jnp.concatenate([b, b2]), "rep", 1)
    return near, jnp.concatenate([a23, b13])


def gather_plan(tokens, expert_of, w_gate, w_up, d_hidden):
    expert_count = lax.axis_size("exp")
    replica_count = lax.axis_size("rep")
    capacity = d_hidden.shape[3]
    half = tokens.shape[1] // 2
    slots_all = expert_count * capacity
    me, core = lax.axis_index("exp"), lax.axis_index("shard")
    gate_rows, up_rows = w_gate[0], w_up[0]

    order = lax.rem(me - jnp.arange(expert_count, dtype=jnp.int32) + expert_count, expert_count)
    cotan = d_hidden[0, 0][order].reshape(slots_all, -1)
    cotan_near, cotan_far = gather_rep(cotan)

    placing = placement(targets(expert_of, expert_count, capacity, me), slots_all)
    mine = lax.dynamic_slice_in_dim(tokens, core * half, half, axis=1)
    packed = dot(placing, mine, MATMUL).astype(BF16)
    blocks = [packed[k * capacity : (k + 1) * capacity] for k in range(expert_count)]
    arrived = [blocks[0]] + [turned(blocks[k], "exp", k) for k in range(1, expert_count)]
    rows = jnp.concatenate(arrived)
    near, far = gather_rep(rows)

    def whole(own):
        other = across(own, "shard", 1)
        return jnp.where(
            core == 0,
            jnp.concatenate([own, other], axis=1),
            jnp.concatenate([other, own], axis=1),
        )

    def back(own, cotan):
        full = whole(own)
        gate_act, up_act = dot(full, gate_rows, LAST), dot(full, up_rows, LAST)
        sigma, d_gate, d_up = gradients(gate_act, up_act, cotan)
        return full, gate_act * sigma * up_act, d_gate, d_up

    full, hidden, d_gate, d_up = back(rows, cotan)
    hidden = hidden.astype(BF16).reshape(d_hidden.shape[2:])[order]
    term = dot(d_gate, gate_rows, MATMUL) + dot(d_up, up_rows, MATMUL)
    left, right = term[:, :half], term[:, half:]
    kept = jnp.where(core == 0, left, right)
    sent = jnp.where(core == 0, right, left).astype(BF16)
    d_packed = (kept + across(sent, "shard", 1).astype(F32)).astype(BF16)
    pieces = [d_packed[k * capacity : (k + 1) * capacity] for k in range(expert_count)]
    returned = [pieces[0]] + [turned(pieces[k], "exp", -k) for k in range(1, expert_count)]
    d_tokens = dot(placing, jnp.concatenate(returned), FIRST).astype(BF16)

    grad_gate, grad_up = dot(d_gate, full, FIRST), dot(d_up, full, FIRST)
    for own, cotan_part in ((near, cotan_near), (far, cotan_far)):
        full, _, d_gate, d_up = back(own, cotan_part)
        grad_gate = grad_gate + dot(d_gate, full, FIRST)
        grad_up = grad_up + dot(d_up, full, FIRST)
    scale = 1.0 / replica_count
    grad_gate = (grad_gate * scale).astype(BF16)[None]
    grad_up = (grad_up * scale).astype(BF16)[None]
    return hidden.reshape(d_hidden.shape), d_tokens, grad_gate, grad_up


def local(tokens, expert_of, w_gate, w_up, d_hidden):
    replica_count, shard_count = lax.axis_size("rep"), lax.axis_size("shard")
    slots_all = d_hidden.shape[2] * d_hidden.shape[3]
    hidden_width, feature_width = w_gate.shape[1:]
    gathered = slots_all * (feature_width // shard_count + hidden_width) * replica_count
    reduced = 4 * hidden_width * feature_width
    if replica_count == 4 and shard_count == 2 and gathered < reduced:
        return gather_plan(tokens, expert_of, w_gate, w_up, d_hidden)
    return reduce_plan(tokens, expert_of, w_gate, w_up, d_hidden)


def solution(mesh):
    in_specs = (
        P(("rep", "exp"), None),
        P(("rep", "exp"), None),
        P("exp", "shard", None),
        P("exp", "shard", None),
        P("rep", "exp", None, None, "shard"),
    )
    out_specs = (
        P("rep", "exp", None, None, "shard"),
        P(("rep", "exp"), "shard"),
        P("exp", "shard", None),
        P("exp", "shard", None),
    )
    return jax.shard_map(local, mesh=mesh, in_specs=in_specs, out_specs=out_specs, check_vma=False)
```

```python
import functools

import jax
import jax.numpy as jnp
from jax import lax
from jax.experimental import pallas as pl
from jax.experimental.pallas import tpu as pltpu
from jax.sharding import PartitionSpec as P

BF16 = jnp.bfloat16
F32 = jnp.float32
LAST = (((1,), (1,)), ((), ()))
FIRST = (((0,), (0,)), ((), ()))
MATMUL = (((1,), (0,)), ((), ()))


def dot(a, b, dims):
    return lax.dot_general(a, b, dims, preferred_element_type=F32)


def targets(expert_of, expert_count, capacity, first):
    routed = expert_of[:, 0]
    chosen = (routed[:, None] == jnp.arange(expert_count, dtype=jnp.int32)[None, :]).astype(
        jnp.int32
    )
    slot_index = jnp.sum(chosen * (jnp.cumsum(chosen, axis=0) - 1), axis=1)
    return lax.rem(routed - first + expert_count, expert_count) * capacity + slot_index


def placement(target, slots_all):
    return (jnp.arange(slots_all, dtype=jnp.int32)[:, None] == target[None, :]).astype(BF16)


def gradients(gate_act, up_act, cotan):
    sigma = jax.nn.sigmoid(gate_act)
    cotan = cotan.astype(F32)
    d_gate = (cotan * up_act * sigma * (1.0 + gate_act * (1.0 - sigma))).astype(BF16)
    d_up = (cotan * gate_act * sigma).astype(BF16)
    return sigma, d_gate, d_up


def reduce_plan(tokens, expert_of, w_gate, w_up, d_hidden):
    expert_count = lax.axis_size("exp")
    replica_count = lax.axis_size("rep")
    capacity = d_hidden.shape[3]
    feature_width = tokens.shape[1]
    slots_all = expert_count * capacity
    placing = placement(targets(expert_of, expert_count, capacity, 0), slots_all)
    packed = dot(placing, tokens, MATMUL).astype(BF16)
    arrived = lax.all_to_all(
        packed.reshape(expert_count, capacity, feature_width), "exp", 0, 0, tiled=True
    )
    rows = arrived.reshape(slots_all, feature_width)
    gate_act, up_act = dot(rows, w_gate[0], LAST), dot(rows, w_up[0], LAST)
    cotan = d_hidden.reshape(slots_all, w_gate.shape[1])
    sigma, d_gate, d_up = gradients(gate_act, up_act, cotan)
    hidden = (gate_act * sigma * up_act).astype(BF16)

    def reduced(d_act):
        total = lax.psum(dot(d_act, rows, FIRST).astype(BF16), "rep").astype(F32)
        return (total * (1.0 / replica_count)).astype(BF16)[None]

    term = dot(d_gate, w_gate[0], MATMUL) + dot(d_up, w_up[0], MATMUL)
    outgoing = term.astype(BF16).reshape(expert_count, capacity, feature_width)
    returned = lax.all_to_all(outgoing, "exp", 0, 0, tiled=True)
    unpacked = dot(placing, returned.reshape(slots_all, feature_width), FIRST)
    d_tokens = lax.psum_scatter(unpacked.astype(BF16), "shard", scatter_dimension=1, tiled=True)
    return hidden.reshape(d_hidden.shape), d_tokens, reduced(d_gate), reduced(d_up)


def across(x, axis, bit):
    size = lax.axis_size(axis)
    return lax.ppermute(x, axis, [(i, i ^ bit) for i in range(size)])


def turned(x, axis, step):
    size = lax.axis_size(axis)
    return lax.ppermute(x, axis, [(i, (i + step) % size) for i in range(size)])


SMEM = pl.BlockSpec(memory_space=pltpu.SMEM)
VMEM = pl.BlockSpec(memory_space=pltpu.VMEM)
ANY = pl.BlockSpec(memory_space=pl.ANY)


def call(kernel, ins, outs, args, scratch=(), flops=0, name=None):
    moved = sum(a.size * a.dtype.itemsize for a in args)
    moved += sum(o.size * o.dtype.itemsize for o in outs)
    return pl.pallas_call(
        kernel,
        in_specs=ins,
        out_specs=[VMEM] * len(outs),
        out_shape=outs,
        scratch_shapes=list(scratch),
        compiler_params=pltpu.CompilerParams(vmem_limit_bytes=48 << 20),
        cost_estimate=pl.CostEstimate(flops=flops, transcendentals=0, bytes_accessed=moved),
        name=name,
    )(*args)


def like(*shape, dtype=BF16):
    return jax.ShapeDtypeStruct(shape, dtype)


def place_rows(expert_ref, count, capacity, first):
    tokens = expert_ref.shape[0]
    routed = jnp.transpose(jnp.broadcast_to(expert_ref[...], (tokens, tokens)))
    rows = lax.broadcasted_iota(jnp.int32, (tokens, tokens), 0)
    columns = lax.broadcasted_iota(jnp.int32, (tokens, tokens), 1)
    chosen = routed == rows
    before = dot(chosen.astype(BF16), (rows < columns).astype(BF16), MATMUL)
    slot = jnp.sum(jnp.where(chosen, before, 0.0), axis=0, keepdims=True).astype(jnp.int32)
    turn = routed[:1] - first
    target = jnp.where(turn < 0, turn + count, turn) * capacity + slot
    slots = lax.broadcasted_iota(jnp.int32, (count * capacity, tokens), 0)
    return (slots == target).astype(BF16)


def pack_kernel(count, capacity, ids, expert_ref, tokens_ref, *outs):
    half = tokens_ref.shape[1] // 2
    core = ids[1]
    placing = place_rows(expert_ref, count, capacity, ids[0])
    mine = tokens_ref[:, pl.ds(pl.multiple_of(core * half, 128), half)]
    theirs = tokens_ref[:, pl.ds(pl.multiple_of((1 - core) * half, 128), half)]
    packed = dot(placing, mine, MATMUL).astype(BF16)
    for k in range(count):
        outs[k][...] = packed[k * capacity : (k + 1) * capacity]
    outs[count][...] = dot(placing[:capacity], theirs, MATMUL).astype(BF16)


def unpack_kernel(count, capacity, ids, expert_ref, *refs):
    *pieces, out = refs
    placing = place_rows(expert_ref, count, capacity, ids[0])
    rows = jnp.concatenate([p[...] for p in pieces])
    out[...] = dot(placing, rows, FIRST).astype(BF16)


def sum_kernel(count, kept_ref, got_ref, *outs):
    capacity = kept_ref.shape[0] // count
    for k in range(count):
        at = pl.ds(k * capacity, capacity)
        outs[k][...] = (kept_ref[at].astype(F32) + got_ref[at].astype(F32)).astype(BF16)


def fill(pieces, others, full, core, sem):
    half = full.shape[1] // 2
    copies, start = [], 0
    for piece, other in zip(pieces, others):
        at = pl.ds(start, piece.shape[0])
        for ref, side in ((piece, core), (other, 1 - core)):
            columns = pl.ds(pl.multiple_of(side * half, 128), half)
            copies.append(pltpu.make_async_copy(ref, full.at[at, columns], sem.at[0]))
        start += piece.shape[0]
    return copies


def own_kernel(count, ids, *refs):
    pieces, others = refs[:count], refs[count : 2 * count]
    cotan_ref, gate_ref, up_ref = refs[2 * count : 2 * count + 3]
    full, d_gate_ref, d_up_ref, hidden_ref, kept_ref, sent_ref, sem = refs[2 * count + 3 :]
    me, core = ids[0], ids[1]
    capacity, half = pieces[0].shape[0], full.shape[1] // 2
    copies = fill(pieces, others, full, core, sem)
    for c in copies:
        c.start()
    for c in copies:
        c.wait()
    rows = full[...]
    gate_act, up_act = dot(rows, gate_ref[...], LAST), dot(rows, up_ref[...], LAST)
    for k in range(count):
        at = slice(k * capacity, (k + 1) * capacity)
        source = lax.rem(me - k + count, count)
        gate, up = gate_act[at], up_act[at]
        sigma, d_gate, d_up = gradients(gate, up, cotan_ref[source])
        hidden_ref[source] = (gate * sigma * up).astype(BF16)
        d_gate_ref[at] = d_gate
        d_up_ref[at] = d_up
    for side, out in ((1 - core, sent_ref), (core, kept_ref)):
        columns = pl.ds(pl.multiple_of(side * half, 128), half)
        term = dot(d_gate_ref[...], gate_ref[:, columns], MATMUL)
        term += dot(d_up_ref[...], up_ref[:, columns], MATMUL)
        out[...] = term.astype(BF16)


def part_kernel(count, blocks, ids, *refs):
    n = 2 * len(blocks)
    pieces, others = refs[:n], refs[n : 2 * n]
    cotans, (gate_ref, up_ref) = refs[2 * n : 2 * n + 3], refs[2 * n + 3 : 2 * n + 5]
    full, d_gate_ref, d_up_ref, sem = refs[2 * n + 5 :]
    me, core = ids[0], ids[1]
    copies = fill(pieces, others, full, core, sem)
    for c in copies:
        c.start()
    for c in copies:
        c.wait()
    rows = full[...]
    gate_act, up_act = dot(rows, gate_ref[...], LAST), dot(rows, up_ref[...], LAST)
    start, capacity = 0, pieces[0].shape[0]
    for k in blocks:
        source = lax.rem(me - k + count, count)
        for group in (k % 2, 1 - k % 2, 2):
            at = slice(start, start + capacity)
            _, d_gate, d_up = gradients(gate_act[at], up_act[at], cotans[group][source])
            d_gate_ref[at] = d_gate
            d_up_ref[at] = d_up
            start += capacity


def grad_kernel(scale, n, *refs):
    fulls, gates, ups = refs[:n], refs[n : 2 * n], refs[2 * n : 3 * n]
    for parts, out in ((gates, refs[3 * n]), (ups, refs[3 * n + 1])):
        total = sum(dot(d[...], full[...], FIRST) for d, full in zip(parts, fulls))
        out[...] = (total * scale).astype(BF16)


def gather_plan(tokens, expert_of, w_gate, w_up, d_hidden):
    count = lax.axis_size("exp")
    replica_count = lax.axis_size("rep")
    capacity = d_hidden.shape[3]
    width = tokens.shape[1]
    half = width // 2
    slots_all = count * capacity
    hidden_width = w_gate.shape[1]
    gate_rows, up_rows = w_gate[0], w_up[0]
    ids = jnp.stack([lax.axis_index("exp"), lax.axis_index("shard")]).astype(jnp.int32)
    cotan = d_hidden[0, 0]

    piece = like(capacity, half)
    *blocks, other = call(
        functools.partial(pack_kernel, count, capacity),
        [SMEM, VMEM, VMEM],
        [piece] * (count + 1),
        [ids, expert_of, tokens],
        flops=2 * tokens.size * slots_all,
        name="pack",
    )
    rows = [blocks[0]] + [turned(blocks[k], "exp", k) for k in range(1, count)]
    cotans = [across(cotan, "rep", bit) for bit in (1, 2, 3)]
    others = [other] + [across(r, "shard", 1) for r in rows[1:]]

    full, d_gate, d_up, hidden, kept, sent = call(
        functools.partial(own_kernel, count),
        [SMEM] + [ANY] * (2 * count) + [VMEM] * 3,
        [like(slots_all, width)]
        + [like(slots_all, hidden_width)] * 2
        + [like(count, capacity, hidden_width)]
        + [like(slots_all, half)] * 2,
        [ids, *rows, *others, cotan, gate_rows, up_rows],
        scratch=[pltpu.SemaphoreType.DMA((1,))],
        flops=8 * slots_all * width * hidden_width,
        name="own",
    )
    got = across(sent, "shard", 1)
    returns = call(
        functools.partial(sum_kernel, count), [VMEM] * 2, [piece] * count, [kept, got], name="sum"
    )
    returned = [returns[0]] + [turned(returns[k], "exp", -k) for k in range(1, count)]
    (d_tokens,) = call(
        functools.partial(unpack_kernel, count, capacity),
        [SMEM, VMEM] + [VMEM] * count,
        [like(tokens.shape[0], half)],
        [ids, expert_of, *returned],
        flops=2 * slots_all * tokens.shape[0] * half,
        name="unpack",
    )

    fulls, gates, ups = [full], [d_gate], [d_up]
    for pair in ((0, 1), (2, 3)):
        pieces = []
        for k in pair:
            near = across(rows[k], "rep", 1 + k % 2)
            far = across(jnp.concatenate([rows[k], near]), "rep", 2 - k % 2)
            pieces += [near, far]
        count_rows = sum(p.shape[0] for p in pieces)
        full, d_gate, d_up = call(
            functools.partial(part_kernel, count, pair),
            [SMEM] + [ANY] * (2 * len(pieces)) + [VMEM] * 5,
            [like(count_rows, width)] + [like(count_rows, hidden_width)] * 2,
            [ids, *pieces, *[across(p, "shard", 1) for p in pieces], *cotans, gate_rows, up_rows],
            scratch=[pltpu.SemaphoreType.DMA((1,))],
            flops=4 * count_rows * width * hidden_width,
            name="part",
        )
        fulls.append(full)
        gates.append(d_gate)
        ups.append(d_up)
    grad_gate, grad_up = call(
        functools.partial(grad_kernel, 1.0 / replica_count, len(fulls)),
        [VMEM] * (3 * len(fulls)),
        [like(hidden_width, width)] * 2,
        [*fulls, *gates, *ups],
        flops=4 * replica_count * slots_all * width * hidden_width,
        name="grads",
    )
    return hidden.reshape(d_hidden.shape), d_tokens, grad_gate[None], grad_up[None]


def local(tokens, expert_of, w_gate, w_up, d_hidden):
    replica_count, shard_count = lax.axis_size("rep"), lax.axis_size("shard")
    slots_all = d_hidden.shape[2] * d_hidden.shape[3]
    hidden_width, feature_width = w_gate.shape[1:]
    gathered = slots_all * (feature_width // shard_count + hidden_width) * replica_count
    reduced = 4 * hidden_width * feature_width
    if replica_count == 4 and shard_count == 2 and lax.axis_size("exp") == 4 and gathered < reduced:
        return gather_plan(tokens, expert_of, w_gate, w_up, d_hidden)
    return reduce_plan(tokens, expert_of, w_gate, w_up, d_hidden)


def solution(mesh):
    in_specs = (
        P(("rep", "exp"), None),
        P(("rep", "exp"), None),
        P("exp", "shard", None),
        P("exp", "shard", None),
        P("rep", "exp", None, None, "shard"),
    )
    out_specs = (
        P("rep", "exp", None, None, "shard"),
        P(("rep", "exp"), "shard"),
        P("exp", "shard", None),
        P("exp", "shard", None),
    )
    return jax.shard_map(local, mesh=mesh, in_specs=in_specs, out_specs=out_specs, check_vma=False)
```

```python
import functools

import jax
import jax.numpy as jnp
from jax import lax
from jax.experimental import pallas as pl
from jax.experimental.pallas import tpu as pltpu
from jax.sharding import PartitionSpec as P

BF16 = jnp.bfloat16
F32 = jnp.float32
LAST = (((1,), (1,)), ((), ()))
FIRST = (((0,), (0,)), ((), ()))
MATMUL = (((1,), (0,)), ((), ()))


def dot(a, b, dims):
    return lax.dot_general(a, b, dims, preferred_element_type=F32)


def targets(expert_of, expert_count, capacity, first):
    routed = expert_of[:, 0]
    chosen = (routed[:, None] == jnp.arange(expert_count, dtype=jnp.int32)[None, :]).astype(
        jnp.int32
    )
    slot_index = jnp.sum(chosen * (jnp.cumsum(chosen, axis=0) - 1), axis=1)
    return lax.rem(routed - first + expert_count, expert_count) * capacity + slot_index


def placement(target, slots_all):
    return (jnp.arange(slots_all, dtype=jnp.int32)[:, None] == target[None, :]).astype(BF16)


def gradients(gate_act, up_act, cotan):
    sigma = jax.nn.sigmoid(gate_act)
    cotan = cotan.astype(F32)
    d_gate = (cotan * up_act * sigma * (1.0 + gate_act * (1.0 - sigma))).astype(BF16)
    d_up = (cotan * gate_act * sigma).astype(BF16)
    return sigma, d_gate, d_up


def reduce_plan(tokens, expert_of, w_gate, w_up, d_hidden):
    expert_count = lax.axis_size("exp")
    replica_count = lax.axis_size("rep")
    capacity = d_hidden.shape[3]
    feature_width = tokens.shape[1]
    slots_all = expert_count * capacity
    placing = placement(targets(expert_of, expert_count, capacity, 0), slots_all)
    packed = dot(placing, tokens, MATMUL).astype(BF16)
    arrived = lax.all_to_all(
        packed.reshape(expert_count, capacity, feature_width), "exp", 0, 0, tiled=True
    )
    rows = arrived.reshape(slots_all, feature_width)
    gate_act, up_act = dot(rows, w_gate[0], LAST), dot(rows, w_up[0], LAST)
    cotan = d_hidden.reshape(slots_all, w_gate.shape[1])
    sigma, d_gate, d_up = gradients(gate_act, up_act, cotan)
    hidden = (gate_act * sigma * up_act).astype(BF16)

    def reduced(d_act):
        total = lax.psum(dot(d_act, rows, FIRST).astype(BF16), "rep").astype(F32)
        return (total * (1.0 / replica_count)).astype(BF16)[None]

    term = dot(d_gate, w_gate[0], MATMUL) + dot(d_up, w_up[0], MATMUL)
    outgoing = term.astype(BF16).reshape(expert_count, capacity, feature_width)
    returned = lax.all_to_all(outgoing, "exp", 0, 0, tiled=True)
    unpacked = dot(placing, returned.reshape(slots_all, feature_width), FIRST)
    d_tokens = lax.psum_scatter(unpacked.astype(BF16), "shard", scatter_dimension=1, tiled=True)
    return hidden.reshape(d_hidden.shape), d_tokens, reduced(d_gate), reduced(d_up)


def across(x, axis, bit):
    size = lax.axis_size(axis)
    return lax.ppermute(x, axis, [(i, i ^ bit) for i in range(size)])


def turned(x, axis, step):
    size = lax.axis_size(axis)
    return lax.ppermute(x, axis, [(i, (i + step) % size) for i in range(size)])


VMEM = pl.BlockSpec(memory_space=pltpu.VMEM)
ANY = pl.BlockSpec(memory_space=pl.ANY)
HBM = pl.BlockSpec(memory_space=pltpu.HBM)


def call(kernel, ins, outs, args, scratch=(), name=None, limit=24, flops=1):
    return pl.pallas_call(
        kernel,
        in_specs=ins,
        out_specs=[VMEM] * len(outs),
        out_shape=outs,
        scratch_shapes=list(scratch),
        compiler_params=pltpu.CompilerParams(vmem_limit_bytes=limit << 20),
        cost_estimate=pl.CostEstimate(flops=flops, transcendentals=0, bytes_accessed=1),
        name=name,
    )(*args)


def like(*shape, dtype=BF16):
    return jax.ShapeDtypeStruct(shape, dtype)


def after(values, *earlier):
    held = lax.optimization_barrier((tuple(values), earlier))
    return list(held[0])


def place_rows(expert_ref, capacity):
    count, first = lax.axis_size("exp"), lax.axis_index("exp")
    tokens = expert_ref.shape[1]
    routed = jnp.broadcast_to(expert_ref[...], (tokens, tokens))
    rows = lax.broadcasted_iota(jnp.int32, (tokens, tokens), 0)
    columns = lax.broadcasted_iota(jnp.int32, (tokens, tokens), 1)
    chosen = routed == rows
    before = dot(chosen.astype(BF16), (rows < columns).astype(BF16), MATMUL)
    slot = jnp.sum(jnp.where(chosen, before, 0.0), axis=0, keepdims=True).astype(jnp.int32)
    turn = routed[:1] - first
    target = jnp.where(turn < 0, turn + count, turn) * capacity + slot
    slots = lax.broadcasted_iota(jnp.int32, (count * capacity, tokens), 0)
    return (slots == target).astype(BF16)


def side_of(core, half):
    return pl.ds(pl.multiple_of(core * half, 128), half)


def load_kernel(a_ref, b_ref, a_out, b_out, sem):
    copies = [
        pltpu.make_async_copy(a_ref, a_out, sem.at[0]),
        pltpu.make_async_copy(b_ref, b_out, sem.at[1]),
    ]
    for c in copies:
        c.start()
    for c in copies:
        c.wait()


def pack_kernel(capacity, expert_hbm, tokens_hbm, *refs):
    *outs, experts, mine, theirs, sem = refs
    count, core = lax.axis_size("exp"), lax.axis_index("shard")
    half = mine.shape[1]
    first = pltpu.make_async_copy(expert_hbm, experts, sem.at[0])
    second = pltpu.make_async_copy(tokens_hbm.at[:, side_of(core, half)], mine, sem.at[1])
    third = pltpu.make_async_copy(tokens_hbm.at[:, side_of(1 - core, half)], theirs, sem.at[2])
    first.start()
    second.start()
    third.start()
    first.wait()
    placing = place_rows(experts, capacity)
    second.wait()
    packed = dot(placing, mine[...], MATMUL).astype(BF16)
    for k in range(count):
        outs[k][...] = packed[k * capacity : (k + 1) * capacity]
    third.wait()
    outs[count][...] = dot(placing[:capacity], theirs[...], MATMUL).astype(BF16)


def unpack_kernel(capacity, expert_ref, *refs):
    *pieces, out = refs
    rows = jnp.concatenate([p[...] for p in pieces])
    out[...] = dot(place_rows(expert_ref, capacity), rows, FIRST).astype(BF16)


def sum_kernel(kept_ref, *refs):
    n = len(refs) // 2
    capacity = refs[0].shape[0]
    for k, (got, out) in enumerate(zip(refs[:n], refs[n:])):
        at = pl.ds(k * capacity, capacity)
        out[...] = (kept_ref[at].astype(F32) + got[...].astype(F32)).astype(BF16)


def fill(pieces, others, full, sem):
    core, half = lax.axis_index("shard"), full.shape[1] // 2
    copies, start = [], 0
    for piece, other in zip(pieces, others):
        at = pl.ds(start, piece.shape[0])
        for ref, side in ((piece, core), (other, 1 - core)):
            copies.append(pltpu.make_async_copy(ref, full.at[at, side_of(side, half)], sem.at[0]))
        start += piece.shape[0]
    for c in copies:
        c.start()
    for c in copies:
        c.wait()


def source_of(k):
    count = lax.axis_size("exp")
    return lax.rem(lax.axis_index("exp") - k + count, count)


def own_kernel(blocks, earlier, n, *refs):
    pieces, others = refs[:n], refs[n : 2 * n]
    cotan_ref, gate_ref, up_ref = refs[2 * n : 2 * n + 3]
    refs = refs[2 * n + 3 :]
    full, d_gate_ref, d_up_ref, kept_ref, *sent_refs = refs[len(refs) - 6 - len(blocks) : -2]
    hidden_ref, sem = refs[-2:]
    core, half = lax.axis_index("shard"), full.shape[1] // 2
    capacity = cotan_ref.shape[1]
    fill(pieces, others, full, sem)
    rows = full[...]
    gate_act, up_act = dot(rows, gate_ref[...], LAST), dot(rows, up_ref[...], LAST)
    for i, k in enumerate(blocks):
        at = slice(i * capacity, (i + 1) * capacity)
        gate, up = gate_act[at], up_act[at]
        sigma, d_gate, d_up = gradients(gate, up, cotan_ref[source_of(k)])
        hidden = (gate * sigma * up).astype(BF16)
        if len(blocks) + len(earlier) == lax.axis_size("exp"):
            hidden_ref[source_of(k)] = hidden
        else:
            hidden_ref[i] = hidden
        d_gate_ref[at] = d_gate
        d_up_ref[at] = d_up
    for i, k in enumerate(earlier):
        hidden_ref[source_of(k)] = refs[0][i]
    for side, outs in ((1 - core, sent_refs), (core, [kept_ref])):
        term = dot(d_gate_ref[...], gate_ref[:, side_of(side, half)], MATMUL)
        term += dot(d_up_ref[...], up_ref[:, side_of(side, half)], MATMUL)
        start = 0
        for out in outs:
            out[...] = term[start : start + out.shape[0]].astype(BF16)
            start += out.shape[0]


def part_kernel(plan, *refs):
    n = (len(refs) - 9) // 2
    pieces, others = refs[:n], refs[n : 2 * n]
    near, far, zero, gate_ref, up_ref, full, d_gate_ref, d_up_ref, sem = refs[2 * n :]
    fill(pieces, others, full, sem)
    rows = full[...]
    gate_act, up_act = dot(rows, gate_ref[...], LAST), dot(rows, up_ref[...], LAST)
    capacity = near.shape[1]
    for i, (k, group) in enumerate(plan):
        at = slice(i * capacity, (i + 1) * capacity)
        source = source_of(k)
        cotan = near[source] if group == 2 else far[0 if group == 1 else 1, source]
        _, d_gate, d_up = gradients(gate_act[at], up_act[at], cotan)
        d_gate_ref[at] = d_gate
        d_up_ref[at] = d_up


def grad_kernel(scale, n, *refs):
    fulls, gates, ups = refs[:n], refs[n : 2 * n], refs[2 * n : 3 * n]
    *earlier, gate_out, up_out = refs[3 * n :]
    for i, (parts, out) in enumerate(((gates, gate_out), (ups, up_out))):
        total = sum(dot(d[...], full[...], FIRST) for d, full in zip(parts, fulls))
        if earlier:
            total += earlier[i][...]
        out[...] = (total * scale).astype(out.dtype)


def swap(x):
    return across(x, "shard", 1)


def gather_plan(tokens, expert_of, w_gate, w_up, d_hidden):
    count = lax.axis_size("exp")
    capacity = d_hidden.shape[3]
    width = tokens.shape[1]
    half = width // 2
    hidden_width = w_gate.shape[1]
    gate_rows, up_rows, cotan = w_gate[0], w_up[0], d_hidden[0, 0]
    experts = expert_of.reshape(1, -1)
    sem = [pltpu.SemaphoreType.DMA((1,))]
    piece = like(capacity, half)

    def own(pair, rows, others, earlier, hidden):
        n = len(pair) * capacity
        return call(
            functools.partial(own_kernel, pair, earlier, len(rows)),
            [ANY] * (2 * len(rows)) + [VMEM] * (3 + len(hidden)),
            [like(n, width)]
            + [like(n, hidden_width)] * 2
            + [like(n, half)] + [piece] * len(pair)
            + [like(len(pair) + len(earlier), capacity, hidden_width)],
            [*rows, *others, cotan, gate_rows, up_rows, *hidden],
            scratch=sem,
            name="own",
        )

    def part(plan, pieces, near, far):
        n = sum(p.shape[0] for p in pieces)
        return call(
            functools.partial(part_kernel, plan),
            [ANY] * (2 * len(pieces)) + [VMEM] * 5,
            [like(n, width)] + [like(n, hidden_width)] * 2,
            [*pieces, *[swap(p) for p in pieces], near, far, near, gate_rows, up_rows],
            scratch=sem,
            name="part",
        )

    def add(kept, got):
        n = len(got)
        return call(sum_kernel, [VMEM] * (1 + n), [piece] * n, [kept, *got], name="sum")

    *blocks, other = call(
        functools.partial(pack_kernel, capacity),
        [HBM, HBM],
        [piece] * (count + 1),
        [pltpu.with_memory_space_constraint(x, pltpu.HBM) for x in (experts, tokens)],
        scratch=[
            pltpu.VMEM(experts.shape, jnp.int32),
            pltpu.VMEM((tokens.shape[0], half), BF16),
            pltpu.VMEM((tokens.shape[0], half), BF16),
            pltpu.SemaphoreType.DMA((3,)),
        ],
        name="pack",
    )
    c0 = blocks[0]
    z1, z2, z3 = (turned(blocks[k], "exp", k) for k in (1, 2, 3))
    (cotan_sent,) = after([cotan], c0)
    c0_near = across(c0, "rep", 1)
    cotan_near = across(cotan_sent, "rep", 2)
    gate_rows, up_rows = call(
        load_kernel,
        [HBM] * 2,
        [like(hidden_width, width)] * 2,
        after([pltpu.with_memory_space_constraint(x, pltpu.HBM) for x in (gate_rows, up_rows)], c0),
        scratch=[pltpu.SemaphoreType.DMA((2,))],
        name="load",
    )
    c0_kept, c0_near_kept = after([c0, c0_near], gate_rows, up_rows)
    c0_both = jnp.concatenate([c0_kept, c0_near_kept])
    cotan_both = jnp.stack([cotan, cotan_near])
    c0_far = across(c0_both, "rep", 2)
    cotan_far = across(cotan_both, "rep", 1)

    z1, z2, z3 = after([z1, z2, z3], c0_both, cotan_both)
    o1, o2, o3 = swap(z1), swap(z2), swap(z3)
    c123 = jnp.concatenate([z1, z2, z3])
    c123_x, c123_y, c123_d = (across(c123, "rep", bit) for bit in (1, 2, 3))
    o1, o2, o3 = after([o1, o2, o3], c0_far, cotan_far)
    full_a, d_gate_a, d_up_a, kept, *sent, hidden = own(
        (0, 1, 2, 3), [c0, z1, z2, z3], [other, o1, o2, o3], (), ()
    )
    r0, r1, r2, r3 = add(kept, [swap(s) for s in sent])
    r1, r2, r3 = turned(r1, "exp", -1), turned(r2, "exp", -2), turned(r3, "exp", -3)
    plan = ((0, 1), (0, 2), (0, 3))
    full_c, d_gate_c, d_up_c = part(plan, [c0_near, c0_far], cotan_near, cotan_far)
    wide = like(hidden_width, width, dtype=F32)
    total_gate, total_up = call(
        functools.partial(grad_kernel, 1.0, 2),
        [VMEM] * 6,
        [wide] * 2,
        [full_a, full_c, d_gate_a, d_gate_c, d_up_a, d_up_c],
        name="grads_near",
        limit=32,
    )
    r2, r3 = after([r2, r3], total_gate)
    (d_tokens,) = call(
        functools.partial(unpack_kernel, capacity),
        [VMEM] * (1 + count),
        [like(tokens.shape[0], half)],
        [experts, r0, r1, r2, r3],
        name="unpack",
    )
    c123_x, c123_y, c123_d = after([c123_x, c123_y, c123_d], d_tokens)
    plan = tuple((k, group) for group in (1, 2, 3) for k in (1, 2, 3))
    full_d, d_gate_d, d_up_d = part(plan, [c123_x, c123_y, c123_d], cotan_near, cotan_far)
    grad_gate, grad_up = call(
        functools.partial(grad_kernel, 1.0 / lax.axis_size("rep"), 1),
        [VMEM] * 5,
        [like(hidden_width, width)] * 2,
        [full_d, d_gate_d, d_up_d, total_gate, total_up],
        name="grads",
        limit=32,
    )
    return hidden.reshape(d_hidden.shape), d_tokens, grad_gate[None], grad_up[None]


def local(tokens, expert_of, w_gate, w_up, d_hidden):
    replica_count, shard_count = lax.axis_size("rep"), lax.axis_size("shard")
    slots_all = d_hidden.shape[2] * d_hidden.shape[3]
    hidden_width, feature_width = w_gate.shape[1:]
    gathered = slots_all * (feature_width // shard_count + hidden_width) * replica_count
    reduced = 4 * hidden_width * feature_width
    if replica_count == 4 and shard_count == 2 and lax.axis_size("exp") == 4 and gathered < reduced:
        return gather_plan(tokens, expert_of, w_gate, w_up, d_hidden)
    return reduce_plan(tokens, expert_of, w_gate, w_up, d_hidden)


def solution(mesh):
    in_specs = (
        P(("rep", "exp"), None),
        P(("rep", "exp"), None),
        P("exp", "shard", None),
        P("exp", "shard", None),
        P("rep", "exp", None, None, "shard"),
    )
    out_specs = (
        P("rep", "exp", None, None, "shard"),
        P(("rep", "exp"), "shard"),
        P("exp", "shard", None),
        P("exp", "shard", None),
    )
    return jax.shard_map(local, mesh=mesh, in_specs=in_specs, out_specs=out_specs, check_vma=False)
```

```python
import functools

import jax
import jax.numpy as jnp
from jax import lax
from jax.experimental import pallas as pl
from jax.experimental.pallas import tpu as pltpu
from jax.sharding import PartitionSpec as P

BF16 = jnp.bfloat16
F32 = jnp.float32
LAST = (((1,), (1,)), ((), ()))
FIRST = (((0,), (0,)), ((), ()))
MATMUL = (((1,), (0,)), ((), ()))


def dot(a, b, dims):
    return lax.dot_general(a, b, dims, preferred_element_type=F32)


def targets(expert_of, expert_count, capacity, first):
    routed = expert_of[:, 0]
    chosen = (routed[:, None] == jnp.arange(expert_count, dtype=jnp.int32)[None, :]).astype(
        jnp.int32
    )
    slot_index = jnp.sum(chosen * (jnp.cumsum(chosen, axis=0) - 1), axis=1)
    return lax.rem(routed - first + expert_count, expert_count) * capacity + slot_index


def placement(target, slots_all):
    return (jnp.arange(slots_all, dtype=jnp.int32)[:, None] == target[None, :]).astype(BF16)


def gradients(gate_act, up_act, cotan):
    sigma = jax.nn.sigmoid(gate_act)
    cotan = cotan.astype(F32)
    d_gate = (cotan * up_act * sigma * (1.0 + gate_act * (1.0 - sigma))).astype(BF16)
    d_up = (cotan * gate_act * sigma).astype(BF16)
    return sigma, d_gate, d_up


def reduce_plan(tokens, expert_of, w_gate, w_up, d_hidden):
    expert_count = lax.axis_size("exp")
    replica_count = lax.axis_size("rep")
    capacity = d_hidden.shape[3]
    feature_width = tokens.shape[1]
    slots_all = expert_count * capacity
    placing = placement(targets(expert_of, expert_count, capacity, 0), slots_all)
    packed = dot(placing, tokens, MATMUL).astype(BF16)
    arrived = lax.all_to_all(
        packed.reshape(expert_count, capacity, feature_width), "exp", 0, 0, tiled=True
    )
    rows = arrived.reshape(slots_all, feature_width)
    gate_act, up_act = dot(rows, w_gate[0], LAST), dot(rows, w_up[0], LAST)
    cotan = d_hidden.reshape(slots_all, w_gate.shape[1])
    sigma, d_gate, d_up = gradients(gate_act, up_act, cotan)
    hidden = (gate_act * sigma * up_act).astype(BF16)

    def reduced(d_act):
        total = lax.psum(dot(d_act, rows, FIRST).astype(BF16), "rep").astype(F32)
        return (total * (1.0 / replica_count)).astype(BF16)[None]

    term = dot(d_gate, w_gate[0], MATMUL) + dot(d_up, w_up[0], MATMUL)
    outgoing = term.astype(BF16).reshape(expert_count, capacity, feature_width)
    returned = lax.all_to_all(outgoing, "exp", 0, 0, tiled=True)
    unpacked = dot(placing, returned.reshape(slots_all, feature_width), FIRST)
    d_tokens = lax.psum_scatter(unpacked.astype(BF16), "shard", scatter_dimension=1, tiled=True)
    return hidden.reshape(d_hidden.shape), d_tokens, reduced(d_gate), reduced(d_up)


def across(x, axis, bit):
    size = lax.axis_size(axis)
    return lax.ppermute(x, axis, [(i, i ^ bit) for i in range(size)])


def turned(x, axis, step):
    size = lax.axis_size(axis)
    return lax.ppermute(x, axis, [(i, (i + step) % size) for i in range(size)])


VMEM = pl.BlockSpec(memory_space=pltpu.VMEM)
ANY = pl.BlockSpec(memory_space=pl.ANY)
HBM = pl.BlockSpec(memory_space=pltpu.HBM)


def call(kernel, ins, outs, args, scratch=(), name=None, limit=24, flops=1, out_spec=VMEM):
    return pl.pallas_call(
        kernel,
        in_specs=ins,
        out_specs=[out_spec] * len(outs),
        out_shape=outs,
        scratch_shapes=list(scratch),
        compiler_params=pltpu.CompilerParams(vmem_limit_bytes=limit << 20),
        cost_estimate=pl.CostEstimate(flops=flops, transcendentals=0, bytes_accessed=1),
        name=name,
    )(*args)


def like(*shape, dtype=BF16):
    return jax.ShapeDtypeStruct(shape, dtype)


def after(values, *earlier):
    held = lax.optimization_barrier((tuple(values), earlier))
    return list(held[0])


def place_rows(expert_ref, capacity):
    count, first = lax.axis_size("exp"), lax.axis_index("exp")
    tokens = expert_ref.shape[1]
    routed = jnp.broadcast_to(expert_ref[...], (tokens, tokens))
    rows = lax.broadcasted_iota(jnp.int32, (tokens, tokens), 0)
    columns = lax.broadcasted_iota(jnp.int32, (tokens, tokens), 1)
    chosen = routed == rows
    before = dot(chosen.astype(BF16), (rows < columns).astype(BF16), MATMUL)
    slot = jnp.sum(jnp.where(chosen, before, 0.0), axis=0, keepdims=True).astype(jnp.int32)
    turn = routed[:1] - first
    target = jnp.where(turn < 0, turn + count, turn) * capacity + slot
    slots = lax.broadcasted_iota(jnp.int32, (count * capacity, tokens), 0)
    return (slots == target).astype(BF16)


def side_of(core, half):
    return pl.ds(pl.multiple_of(core * half, 128), half)


def load_kernel(gate_ref, up_ref, out, sem):
    units = gate_ref.shape[0]
    copies = [
        pltpu.make_async_copy(gate_ref, out.at[:units], sem.at[0]),
        pltpu.make_async_copy(up_ref, out.at[units:], sem.at[1]),
    ]
    for c in copies:
        c.start()
    for c in copies:
        c.wait()


def pack_kernel(capacity, expert_hbm, tokens_hbm, *refs):
    *outs, experts, mine, theirs, sem = refs
    count, core = lax.axis_size("exp"), lax.axis_index("shard")
    half = mine.shape[1]
    first = pltpu.make_async_copy(expert_hbm, experts, sem.at[0])
    second = pltpu.make_async_copy(tokens_hbm.at[:, side_of(core, half)], mine, sem.at[1])
    third = pltpu.make_async_copy(tokens_hbm.at[:, side_of(1 - core, half)], theirs, sem.at[2])
    first.start()
    second.start()
    third.start()
    first.wait()
    placing = place_rows(experts, capacity)
    second.wait()
    packed = dot(placing, mine[...], MATMUL).astype(BF16)
    for k in range(count):
        outs[k][...] = packed[k * capacity : (k + 1) * capacity]
    third.wait()
    outs[count][...] = dot(placing[:capacity], theirs[...], MATMUL).astype(BF16)


def unpack_kernel(capacity, expert_ref, *refs):
    *pieces, out = refs
    rows = jnp.concatenate([p[...] for p in pieces])
    out[...] = dot(place_rows(expert_ref, capacity), rows, FIRST).astype(BF16)


def sum_kernel(kept_ref, *refs):
    got_ref, *outs = refs
    capacity = outs[0].shape[0]
    for k, out in enumerate(outs):
        at = pl.ds(k * capacity, capacity)
        out[...] = (kept_ref[at].astype(F32) + got_ref[at].astype(F32)).astype(BF16)


def fill(pieces, others, full, sem):
    core, half = lax.axis_index("shard"), full.shape[1] // 2
    copies, start = [], 0
    for piece, other in zip(pieces, others):
        at = pl.ds(start, piece.shape[0])
        for ref, side in ((piece, core), (other, 1 - core)):
            copies.append(pltpu.make_async_copy(ref, full.at[at, side_of(side, half)], sem.at[0]))
        start += piece.shape[0]
    for c in copies:
        c.start()
    for c in copies:
        c.wait()


def source_of(k):
    count = lax.axis_size("exp")
    return lax.rem(lax.axis_index("exp") - k + count, count)


def own_kernel(blocks, *refs):
    n = len(blocks)
    pieces, others = refs[:n], refs[n : 2 * n]
    cotan_ref, rows_ref, full, d_ref, kept_ref, sent_ref, hidden_ref, sem = refs[2 * n :]
    core, half = lax.axis_index("shard"), full.shape[1] // 2
    capacity, units = cotan_ref.shape[1:]
    fill(pieces, others, full, sem)
    acts = dot(full[...], rows_ref[...], LAST)
    for i, k in enumerate(blocks):
        at = slice(i * capacity, (i + 1) * capacity)
        gate, up = acts[at, :units], acts[at, units:]
        sigma, d_gate, d_up = gradients(gate, up, cotan_ref[source_of(k)])
        hidden_ref[source_of(k)] = (gate * sigma * up).astype(BF16)
        d_ref[at, :units] = d_gate
        d_ref[at, units:] = d_up
    for side, out in ((1 - core, sent_ref), (core, kept_ref)):
        out[...] = dot(d_ref[...], rows_ref[:, side_of(side, half)], MATMUL).astype(BF16)


def part_kernel(plan, n, *refs):
    pieces, others = refs[:n], refs[n : 2 * n]
    near, far, rows_ref, full, d_ref, sem = refs[2 * n :]
    capacity, units = near.shape[1:]
    fill(pieces, others, full, sem)
    acts = dot(full[...], rows_ref[...], LAST)
    for i, (k, group) in enumerate(plan):
        at = slice(i * capacity, (i + 1) * capacity)
        source = source_of(k)
        cotan = near[source] if group == 2 else far[0 if group == 1 else 1, source]
        _, d_gate, d_up = gradients(acts[at, :units], acts[at, units:], cotan)
        d_ref[at, :units] = d_gate
        d_ref[at, units:] = d_up


def grad_kernel(n, *refs):
    fulls, ds, out = refs[:n], refs[n : 2 * n], refs[2 * n]
    out[...] = sum(dot(d[...], full[...], FIRST) for d, full in zip(ds, fulls))


def last_grad_kernel(scale, n, *refs):
    fulls, ds = refs[:n], refs[n : 2 * n]
    earlier, gate_out, up_out, staged, sem = refs[2 * n :]
    units, quarter, copies = gate_out.shape[0], staged.shape[1] // 4, []
    for i in range(4):
        columns = slice(i * quarter, (i + 1) * quarter)
        total = sum(dot(d[...], full[:, columns], FIRST) for d, full in zip(ds, fulls))
        staged[:, columns] = ((total + earlier[:, columns]) * scale).astype(BF16)
        for j, out in enumerate((gate_out, up_out)):
            copies.append(
                pltpu.make_async_copy(
                    staged.at[j * units : (j + 1) * units, columns],
                    out.at[:, columns],
                    sem.at[i, j],
                )
            )
            copies[-1].start()
    for c in copies:
        c.wait()


def swap(x):
    return across(x, "shard", 1)


def gather_plan(tokens, expert_of, w_gate, w_up, d_hidden):
    count = lax.axis_size("exp")
    capacity = d_hidden.shape[3]
    width = tokens.shape[1]
    half = width // 2
    hidden_width = w_gate.shape[1]
    gate_rows, up_rows, cotan = w_gate[0], w_up[0], d_hidden[0, 0]
    experts = expert_of.reshape(1, -1)
    sem = [pltpu.SemaphoreType.DMA((1,))]
    piece = like(capacity, half)

    def own(pair, rows, others):
        n = len(pair) * capacity
        return call(
            functools.partial(own_kernel, pair),
            [ANY] * (2 * len(rows)) + [VMEM] * 2,
            [like(n, width), like(n, 2 * hidden_width)]
            + [like(n, half)] * 2
            + [like(len(pair), capacity, hidden_width)],
            [*rows, *others, cotan, both_rows],
            scratch=sem,
            name="own",
        )

    def part(plan, pieces, others, near, far):
        n = sum(p.shape[0] for p in pieces)
        return call(
            functools.partial(part_kernel, plan, len(pieces)),
            [ANY] * (2 * len(pieces)) + [VMEM] * 3,
            [like(n, width), like(n, 2 * hidden_width)],
            [*pieces, *others, near, far, both_rows],
            scratch=sem,
            name="part",
        )

    def add(kept, got):
        return call(sum_kernel, [VMEM] * 2, [piece] * count, [kept, got], name="sum")

    *blocks, other = call(
        functools.partial(pack_kernel, capacity),
        [HBM, HBM],
        [piece] * (count + 1),
        [pltpu.with_memory_space_constraint(x, pltpu.HBM) for x in (experts, tokens)],
        scratch=[
            pltpu.VMEM(experts.shape, jnp.int32),
            pltpu.VMEM((tokens.shape[0], half), BF16),
            pltpu.VMEM((tokens.shape[0], half), BF16),
            pltpu.SemaphoreType.DMA((3,)),
        ],
        name="pack",
    )
    c0 = blocks[0]
    z1, z2, z3 = (turned(blocks[k], "exp", k) for k in (1, 2, 3))
    (cotan_sent,) = after([cotan], c0)
    c0_near = across(c0, "rep", 1)
    cotan_near = across(cotan_sent, "rep", 2)
    (both_rows,) = call(
        load_kernel,
        [HBM] * 2,
        [like(2 * hidden_width, width)],
        after([pltpu.with_memory_space_constraint(x, pltpu.HBM) for x in (gate_rows, up_rows)], c0),
        scratch=[pltpu.SemaphoreType.DMA((2,))],
        name="load",
    )
    c0_kept, c0_near_kept = after([c0, c0_near], both_rows)
    c0_both = jnp.concatenate([c0_kept, c0_near_kept])
    cotan_both = jnp.stack([cotan, cotan_near])
    c0_far = across(c0_both, "rep", 2)
    cotan_far = across(cotan_both, "rep", 1)

    z1, z2, z3 = after([z1, z2, z3], c0_both, cotan_both)
    o1, o2, o3 = swap(z1), swap(z2), swap(z3)
    c123 = jnp.concatenate([z1, z2, z3])
    o1, o2, o3 = after([o1, o2, o3], c0_far, cotan_far)
    full_a, d_a, kept, sent, hidden = own((0, 1, 2, 3), [c0, z1, z2, z3], [other, o1, o2, o3])
    c123_sent, c0_near_sent, c0_far_sent = after([c123, c0_near, c0_far], kept)
    c123_x, c123_y = across(c123_sent, "rep", 1), across(c123_sent, "rep", 2)
    c0_others = [swap(c0_near_sent), swap(c0_far_sent)]
    r0, r1, r2, r3 = add(kept, swap(sent))
    r1, r2, r3 = after([r1, r2, r3], *c0_others)
    r1, r2, r3 = turned(r1, "exp", -1), turned(r2, "exp", -2), turned(r3, "exp", -3)

    plan = ((0, 1), (0, 2), (0, 3))
    full_c, d_c = part(plan, [c0_near, c0_far], c0_others, cotan_near, cotan_far)
    (total,) = call(
        functools.partial(grad_kernel, 2),
        [VMEM] * 4,
        [like(2 * hidden_width, width, dtype=F32)],
        [full_a, full_c, d_a, d_c],
        name="grads_near",
        limit=32,
    )
    c123_x, c123_y = after([c123_x, c123_y], total)
    cut = (c123.shape[0] // 2 + 15) // 16 * 16
    far_sent = [across(c123_x[:cut], "rep", 2), across(c123_y[cut:], "rep", 1)]
    (d_tokens,) = call(
        functools.partial(unpack_kernel, capacity),
        [VMEM] * (1 + count),
        [like(tokens.shape[0], half)],
        [experts, r0, r1, r2, r3],
        name="unpack",
        flops=6*10**9,
    )
    (c123_x,), (c123_y,) = after([c123_x], r1), after([c123_y], r2)
    far_sent = after(far_sent, d_tokens)
    plan = tuple((k, group) for group in (1, 2) for k in (1, 2, 3))
    full_d, d_d = part(
        plan, [c123_x, c123_y], [swap(c123_x), swap(c123_y)], cotan_near, cotan_far
    )
    plan = tuple((k, 3) for k in (1, 2, 3))
    full_e, d_e = part(
        plan, far_sent, after([swap(f) for f in far_sent], d_d), cotan_near, cotan_far
    )
    grad_gate, grad_up = call(
        functools.partial(last_grad_kernel, 1.0 / lax.axis_size("rep"), 2),
        [VMEM] * 5,
        [like(hidden_width, width)] * 2,
        [full_d, full_e, d_d, d_e, total],
        scratch=[pltpu.VMEM((2 * hidden_width, width), BF16), pltpu.SemaphoreType.DMA((4, 2))],
        name="grads",
        limit=32,
        out_spec=HBM,
    )
    return hidden.reshape(d_hidden.shape), d_tokens, grad_gate[None], grad_up[None]


def local(tokens, expert_of, w_gate, w_up, d_hidden):
    replica_count, shard_count = lax.axis_size("rep"), lax.axis_size("shard")
    slots_all = d_hidden.shape[2] * d_hidden.shape[3]
    hidden_width, feature_width = w_gate.shape[1:]
    gathered = slots_all * (feature_width // shard_count + hidden_width) * replica_count
    reduced = 4 * hidden_width * feature_width
    if replica_count == 4 and shard_count == 2 and lax.axis_size("exp") == 4 and gathered < reduced:
        return gather_plan(tokens, expert_of, w_gate, w_up, d_hidden)
    return reduce_plan(tokens, expert_of, w_gate, w_up, d_hidden)


def solution(mesh):
    in_specs = (
        P(("rep", "exp"), None),
        P(("rep", "exp"), None),
        P("exp", "shard", None),
        P("exp", "shard", None),
        P("rep", "exp", None, None, "shard"),
    )
    out_specs = (
        P("rep", "exp", None, None, "shard"),
        P(("rep", "exp"), "shard"),
        P("exp", "shard", None),
        P("exp", "shard", None),
    )
    return jax.shard_map(local, mesh=mesh, in_specs=in_specs, out_specs=out_specs, check_vma=False)
```

```python
import functools

import jax
import jax.numpy as jnp
from jax import lax
from jax.experimental import pallas as pl
from jax.experimental.pallas import tpu as pltpu
from jax.sharding import PartitionSpec as P

BF16 = jnp.bfloat16
F32 = jnp.float32
LAST = (((1,), (1,)), ((), ()))
FIRST = (((0,), (0,)), ((), ()))
MATMUL = (((1,), (0,)), ((), ()))


def dot(a, b, dims):
    return lax.dot_general(a, b, dims, preferred_element_type=F32)


def targets(expert_of, expert_count, capacity, first):
    routed = expert_of[:, 0]
    chosen = (routed[:, None] == jnp.arange(expert_count, dtype=jnp.int32)[None, :]).astype(
        jnp.int32
    )
    slot_index = jnp.sum(chosen * (jnp.cumsum(chosen, axis=0) - 1), axis=1)
    return lax.rem(routed - first + expert_count, expert_count) * capacity + slot_index


def placement(target, slots_all):
    return (jnp.arange(slots_all, dtype=jnp.int32)[:, None] == target[None, :]).astype(BF16)


def gradients(gate_act, up_act, cotan):
    sigma = jax.nn.sigmoid(gate_act)
    cotan = cotan.astype(F32)
    d_gate = (cotan * up_act * sigma * (1.0 + gate_act * (1.0 - sigma))).astype(BF16)
    d_up = (cotan * gate_act * sigma).astype(BF16)
    return sigma, d_gate, d_up


def reduce_plan(tokens, expert_of, w_gate, w_up, d_hidden):
    expert_count = lax.axis_size("exp")
    replica_count = lax.axis_size("rep")
    capacity = d_hidden.shape[3]
    feature_width = tokens.shape[1]
    slots_all = expert_count * capacity
    placing = placement(targets(expert_of, expert_count, capacity, 0), slots_all)
    packed = dot(placing, tokens, MATMUL).astype(BF16)
    arrived = lax.all_to_all(
        packed.reshape(expert_count, capacity, feature_width), "exp", 0, 0, tiled=True
    )
    rows = arrived.reshape(slots_all, feature_width)
    gate_act, up_act = dot(rows, w_gate[0], LAST), dot(rows, w_up[0], LAST)
    cotan = d_hidden.reshape(slots_all, w_gate.shape[1])
    sigma, d_gate, d_up = gradients(gate_act, up_act, cotan)
    hidden = (gate_act * sigma * up_act).astype(BF16)

    def reduced(d_act):
        total = lax.psum(dot(d_act, rows, FIRST).astype(BF16), "rep").astype(F32)
        return (total * (1.0 / replica_count)).astype(BF16)[None]

    term = dot(d_gate, w_gate[0], MATMUL) + dot(d_up, w_up[0], MATMUL)
    outgoing = term.astype(BF16).reshape(expert_count, capacity, feature_width)
    returned = lax.all_to_all(outgoing, "exp", 0, 0, tiled=True)
    unpacked = dot(placing, returned.reshape(slots_all, feature_width), FIRST)
    d_tokens = lax.psum_scatter(unpacked.astype(BF16), "shard", scatter_dimension=1, tiled=True)
    return hidden.reshape(d_hidden.shape), d_tokens, reduced(d_gate), reduced(d_up)


def across(x, axis, bit):
    size = lax.axis_size(axis)
    return lax.ppermute(x, axis, [(i, i ^ bit) for i in range(size)])


def turned(x, axis, step):
    size = lax.axis_size(axis)
    return lax.ppermute(x, axis, [(i, (i + step) % size) for i in range(size)])


VMEM = pl.BlockSpec(memory_space=pltpu.VMEM)
ANY = pl.BlockSpec(memory_space=pl.ANY)
HBM = pl.BlockSpec(memory_space=pltpu.HBM)


def call(kernel, ins, outs, args, scratch=(), name=None, limit=24, flops=1, out_spec=VMEM):
    return pl.pallas_call(
        kernel,
        in_specs=ins,
        out_specs=[out_spec] * len(outs),
        out_shape=outs,
        scratch_shapes=list(scratch),
        compiler_params=pltpu.CompilerParams(vmem_limit_bytes=limit << 20),
        cost_estimate=pl.CostEstimate(flops=flops, transcendentals=0, bytes_accessed=1),
        name=name,
    )(*args)


def like(*shape, dtype=BF16):
    return jax.ShapeDtypeStruct(shape, dtype)


def after(values, *earlier):
    held = lax.optimization_barrier((tuple(values), earlier))
    return list(held[0])


def place_rows(expert_ref, capacity):
    count, first = lax.axis_size("exp"), lax.axis_index("exp")
    tokens = expert_ref.shape[1]
    routed = jnp.broadcast_to(expert_ref[...], (tokens, tokens))
    rows = lax.broadcasted_iota(jnp.int32, (tokens, tokens), 0)
    columns = lax.broadcasted_iota(jnp.int32, (tokens, tokens), 1)
    chosen = routed == rows
    before = dot(chosen.astype(BF16), (rows < columns).astype(BF16), MATMUL)
    slot = jnp.sum(jnp.where(chosen, before, 0.0), axis=0, keepdims=True).astype(jnp.int32)
    turn = routed[:1] - first
    target = jnp.where(turn < 0, turn + count, turn) * capacity + slot
    slots = lax.broadcasted_iota(jnp.int32, (count * capacity, tokens), 0)
    return (slots == target).astype(BF16)


def side_of(core, half):
    return pl.ds(pl.multiple_of(core * half, 128), half)


def load_kernel(gate_ref, up_ref, out, sem):
    units = gate_ref.shape[0]
    copies = [
        pltpu.make_async_copy(gate_ref, out.at[:units], sem.at[0]),
        pltpu.make_async_copy(up_ref, out.at[units:], sem.at[1]),
    ]
    for c in copies:
        c.start()
    for c in copies:
        c.wait()


def pack_kernel(capacity, expert_hbm, tokens_hbm, *refs):
    *outs, experts, mine, theirs, sem = refs
    count, core = lax.axis_size("exp"), lax.axis_index("shard")
    half = mine.shape[1]
    first = pltpu.make_async_copy(expert_hbm, experts, sem.at[0])
    second = pltpu.make_async_copy(tokens_hbm.at[:, side_of(core, half)], mine, sem.at[1])
    third = pltpu.make_async_copy(tokens_hbm.at[:, side_of(1 - core, half)], theirs, sem.at[2])
    first.start()
    second.start()
    third.start()
    first.wait()
    placing = place_rows(experts, capacity)
    second.wait()
    packed = dot(placing, mine[...], MATMUL).astype(BF16)
    for k in range(count):
        outs[k][...] = packed[k * capacity : (k + 1) * capacity]
    third.wait()
    outs[count][...] = dot(placing[:capacity], theirs[...], MATMUL).astype(BF16)


def place_kernel(capacity, expert_ref, out):
    out[...] = jnp.transpose(place_rows(expert_ref, capacity))


def unpack_kernel(placing_ref, *refs):
    *pieces, out = refs
    rows = jnp.concatenate([p[...] for p in pieces])
    out[...] = dot(placing_ref[...], rows, MATMUL).astype(BF16)


def sum_kernel(kept_ref, *refs):
    got_ref, *outs = refs
    capacity = outs[0].shape[0]
    for k, out in enumerate(outs):
        at = pl.ds(k * capacity, capacity)
        out[...] = (kept_ref[at].astype(F32) + got_ref[at].astype(F32)).astype(BF16)


def fill(pieces, others, full, sem):
    core, half = lax.axis_index("shard"), full.shape[1] // 2
    copies, start = [], 0
    for piece, other in zip(pieces, others):
        at = pl.ds(start, piece.shape[0])
        for ref, side in ((piece, core), (other, 1 - core)):
            copies.append(pltpu.make_async_copy(ref, full.at[at, side_of(side, half)], sem.at[0]))
        start += piece.shape[0]
    for c in copies:
        c.start()
    for c in copies:
        c.wait()


def source_of(k):
    count = lax.axis_size("exp")
    return lax.rem(lax.axis_index("exp") - k + count, count)


def own_kernel(blocks, *refs):
    n = len(blocks)
    pieces, others = refs[:n], refs[n : 2 * n]
    cotan_ref, rows_ref, full, d_ref, sent_ref, hidden_ref, sem = refs[2 * n :]
    core, half = lax.axis_index("shard"), full.shape[1] // 2
    capacity, units = cotan_ref.shape[1:]
    fill(pieces, others, full, sem)
    acts = dot(full[...], rows_ref[...], LAST)
    for i, k in enumerate(blocks):
        at = slice(i * capacity, (i + 1) * capacity)
        gate, up = acts[at, :units], acts[at, units:]
        sigma, d_gate, d_up = gradients(gate, up, cotan_ref[source_of(k)])
        hidden_ref[source_of(k)] = (gate * sigma * up).astype(BF16)
        d_ref[at, :units] = d_gate
        d_ref[at, units:] = d_up
    theirs = rows_ref[:, side_of(1 - core, half)]
    sent_ref[...] = dot(d_ref[...], theirs, MATMUL).astype(BF16)


def kept_kernel(d_ref, rows_ref, kept_ref):
    mine = rows_ref[:, side_of(lax.axis_index("shard"), kept_ref.shape[1])]
    kept_ref[...] = dot(d_ref[...], mine, MATMUL).astype(BF16)


def part_kernel(plan, n, *refs):
    pieces, others = refs[:n], refs[n : 2 * n]
    near, far, rows_ref, full, d_ref, sem = refs[2 * n :]
    capacity, units = near.shape[1:]
    fill(pieces, others, full, sem)
    acts = dot(full[...], rows_ref[...], LAST)
    for i, (k, group) in enumerate(plan):
        at = slice(i * capacity, (i + 1) * capacity)
        source = source_of(k)
        cotan = near[source] if group == 2 else far[0 if group == 1 else 1, source]
        _, d_gate, d_up = gradients(acts[at, :units], acts[at, units:], cotan)
        d_ref[at, :units] = d_gate
        d_ref[at, units:] = d_up


def grad_kernel(n, *refs):
    fulls, ds, out = refs[:n], refs[n : 2 * n], refs[2 * n]
    out[...] = sum(dot(d[...], full[...], FIRST) for d, full in zip(ds, fulls))


def last_grad_kernel(scale, n, *refs):
    fulls, ds = refs[:n], refs[n : 2 * n]
    earlier, gate_out, up_out, staged, held, sem = refs[2 * n :]
    units, copies, start = gate_out.shape[0], [], 0
    for d in ds:
        held[start : start + d.shape[0]] = d[...]
        start += d.shape[0]
    blocks = sem.shape[0]
    wide = staged.shape[1] // blocks
    for i in range(blocks):
        columns = slice(i * wide, (i + 1) * wide)
        total = dot(held[...], jnp.concatenate([full[:, columns] for full in fulls]), FIRST)
        staged[:, columns] = ((total + earlier[:, columns]) * scale).astype(BF16)
        for j, out in enumerate((gate_out, up_out)):
            copies.append(
                pltpu.make_async_copy(
                    staged.at[j * units : (j + 1) * units, columns],
                    out.at[:, columns],
                    sem.at[i, j],
                )
            )
            copies[-1].start()
    for c in copies:
        c.wait()


def swap(x):
    return across(x, "shard", 1)


def gather_plan(tokens, expert_of, w_gate, w_up, d_hidden):
    count = lax.axis_size("exp")
    capacity = d_hidden.shape[3]
    width = tokens.shape[1]
    half = width // 2
    hidden_width = w_gate.shape[1]
    gate_rows, up_rows, cotan = w_gate[0], w_up[0], d_hidden[0, 0]
    experts = expert_of.reshape(1, -1)
    sem = [pltpu.SemaphoreType.DMA((1,))]
    piece = like(capacity, half)

    def own(pair, rows, others):
        n = len(pair) * capacity
        return call(
            functools.partial(own_kernel, pair),
            [ANY] * (2 * len(rows)) + [VMEM] * 2,
            [like(n, width), like(n, 2 * hidden_width)]
            + [like(n, half)]
            + [like(len(pair), capacity, hidden_width)],
            [*rows, *others, cotan, both_rows],
            scratch=sem,
            name="own",
        )

    def part(plan, pieces, others, near, far):
        n = sum(p.shape[0] for p in pieces)
        return call(
            functools.partial(part_kernel, plan, len(pieces)),
            [ANY] * (2 * len(pieces)) + [VMEM] * 3,
            [like(n, width), like(n, 2 * hidden_width)],
            [*pieces, *others, near, far, both_rows],
            scratch=sem,
            name="part",
        )

    def add(kept, got):
        return call(sum_kernel, [VMEM] * 2, [piece] * count, [kept, got], name="sum")

    *blocks, other = call(
        functools.partial(pack_kernel, capacity),
        [HBM, HBM],
        [piece] * (count + 1),
        [pltpu.with_memory_space_constraint(x, pltpu.HBM) for x in (experts, tokens)],
        scratch=[
            pltpu.VMEM(experts.shape, jnp.int32),
            pltpu.VMEM((tokens.shape[0], half), BF16),
            pltpu.VMEM((tokens.shape[0], half), BF16),
            pltpu.SemaphoreType.DMA((3,)),
        ],
        name="pack",
    )
    c0 = blocks[0]
    z1, z2, z3 = (turned(blocks[k], "exp", k) for k in (1, 2, 3))
    (cotan_sent,) = after([cotan], c0)
    c0_near = across(c0, "rep", 1)
    cotan_near = across(cotan_sent, "rep", 2)
    (both_rows,) = call(
        load_kernel,
        [HBM] * 2,
        [like(2 * hidden_width, width)],
        after([pltpu.with_memory_space_constraint(x, pltpu.HBM) for x in (gate_rows, up_rows)], c0),
        scratch=[pltpu.SemaphoreType.DMA((2,))],
        name="load",
    )
    c0_kept, c0_near_kept = after([c0, c0_near], both_rows)
    c0_both = jnp.concatenate([c0_kept, c0_near_kept])
    cotan_both = jnp.stack([cotan, cotan_near])
    c0_far = across(c0_both, "rep", 2)
    cotan_far = across(cotan_both, "rep", 1)

    z1, z2, z3 = after([z1, z2, z3], c0_both, cotan_both)
    o1, o2, o3 = swap(z1), swap(z2), swap(z3)
    c123 = jnp.concatenate([z1, z2, z3])
    o1, o2, o3 = after([o1, o2, o3], c0_far, cotan_far)
    full_a, d_a, sent, hidden = own((0, 1, 2, 3), [c0, z1, z2, z3], [other, o1, o2, o3])
    (kept,) = call(
        kept_kernel, [VMEM] * 2, [like(count * capacity, half)], [d_a, both_rows], name="kept"
    )
    c123_sent, c0_near_sent, c0_far_sent = after([c123, c0_near, c0_far], sent)
    c123_x, c123_y = across(c123_sent, "rep", 1), across(c123_sent, "rep", 2)
    c0_others = [swap(c0_near_sent), swap(c0_far_sent)]
    r0, r1, r2, r3 = add(kept, swap(sent))
    r1, r2, r3 = turned(r1, "exp", -1), turned(r2, "exp", -2), turned(r3, "exp", -3)

    plan = ((0, 1), (0, 2), (0, 3))
    full_c, d_c = part(plan, [c0_near, c0_far], c0_others, cotan_near, cotan_far)
    (total,) = call(
        functools.partial(grad_kernel, 2),
        [VMEM] * 4,
        [like(2 * hidden_width, width, dtype=F32)],
        [full_a, full_c, d_a, d_c],
        name="grads_near",
        limit=32,
    )
    (placing,) = call(
        functools.partial(place_kernel, capacity),
        [VMEM],
        [like(tokens.shape[0], count * capacity)],
        after([experts], d_c),
        name="place",
    )
    c123_x, c123_y = after([c123_x, c123_y], total, placing)
    cut = (c123.shape[0] // 2 + 15) // 16 * 16
    far_sent = [across(c123_x[:cut], "rep", 2), across(c123_y[cut:], "rep", 1)]
    (d_tokens,) = call(
        unpack_kernel,
        [VMEM] * (1 + count),
        [like(tokens.shape[0], half)],
        [placing, r0, r1, r2, r3],
        name="unpack",
        flops=6*10**9,
    )
    (c123_x,), (c123_y,) = after([c123_x], r1), after([c123_y], r2)
    far_sent = after(far_sent, d_tokens)
    plan = tuple((k, group) for group in (1, 2) for k in (1, 2, 3))
    full_d, d_d = part(
        plan, [c123_x, c123_y], [swap(c123_x), swap(c123_y)], cotan_near, cotan_far
    )
    plan = tuple((k, 3) for k in (1, 2, 3))
    full_e, d_e = part(
        plan, far_sent, after([swap(f) for f in far_sent], d_d), cotan_near, cotan_far
    )
    grad_gate, grad_up = call(
        functools.partial(last_grad_kernel, 1.0 / lax.axis_size("rep"), 2),
        [VMEM] * 5,
        [like(hidden_width, width)] * 2,
        [full_d, full_e, d_d, d_e, total],
        scratch=[
            pltpu.VMEM((2 * hidden_width, width), BF16),
            pltpu.VMEM((d_d.shape[0] + d_e.shape[0], 2 * hidden_width), BF16),
            pltpu.SemaphoreType.DMA((5, 2)),
        ],
        name="grads",
        limit=32,
        out_spec=HBM,
    )
    return hidden.reshape(d_hidden.shape), d_tokens, grad_gate[None], grad_up[None]


def local(tokens, expert_of, w_gate, w_up, d_hidden):
    replica_count, shard_count = lax.axis_size("rep"), lax.axis_size("shard")
    slots_all = d_hidden.shape[2] * d_hidden.shape[3]
    hidden_width, feature_width = w_gate.shape[1:]
    gathered = slots_all * (feature_width // shard_count + hidden_width) * replica_count
    reduced = 4 * hidden_width * feature_width
    if replica_count == 4 and shard_count == 2 and lax.axis_size("exp") == 4 and gathered < reduced:
        return gather_plan(tokens, expert_of, w_gate, w_up, d_hidden)
    return reduce_plan(tokens, expert_of, w_gate, w_up, d_hidden)


def solution(mesh):
    in_specs = (
        P(("rep", "exp"), None),
        P(("rep", "exp"), None),
        P("exp", "shard", None),
        P("exp", "shard", None),
        P("rep", "exp", None, None, "shard"),
    )
    out_specs = (
        P("rep", "exp", None, None, "shard"),
        P(("rep", "exp"), "shard"),
        P("exp", "shard", None),
        P("exp", "shard", None),
    )
    return jax.shard_map(local, mesh=mesh, in_specs=in_specs, out_specs=out_specs, check_vma=False)
```

```python
import functools

import jax
import jax.numpy as jnp
from jax import lax
from jax.experimental import pallas as pl
from jax.experimental.pallas import tpu as pltpu
from jax.sharding import PartitionSpec as P

BF16 = jnp.bfloat16
F32 = jnp.float32
LAST = (((1,), (1,)), ((), ()))
FIRST = (((0,), (0,)), ((), ()))
MATMUL = (((1,), (0,)), ((), ()))


def dot(a, b, dims):
    return lax.dot_general(a, b, dims, preferred_element_type=F32)


def targets(expert_of, expert_count, capacity, first):
    routed = expert_of[:, 0]
    chosen = (routed[:, None] == jnp.arange(expert_count, dtype=jnp.int32)[None, :]).astype(
        jnp.int32
    )
    slot_index = jnp.sum(chosen * (jnp.cumsum(chosen, axis=0) - 1), axis=1)
    return lax.rem(routed - first + expert_count, expert_count) * capacity + slot_index


def placement(target, slots_all):
    return (jnp.arange(slots_all, dtype=jnp.int32)[:, None] == target[None, :]).astype(BF16)


def gradients(gate_act, up_act, cotan):
    sigma = jax.nn.sigmoid(gate_act)
    cotan = cotan.astype(F32)
    d_gate = (cotan * up_act * sigma * (1.0 + gate_act * (1.0 - sigma))).astype(BF16)
    d_up = (cotan * gate_act * sigma).astype(BF16)
    return sigma, d_gate, d_up


def reduce_plan(tokens, expert_of, w_gate, w_up, d_hidden):
    expert_count = lax.axis_size("exp")
    replica_count = lax.axis_size("rep")
    capacity = d_hidden.shape[3]
    feature_width = tokens.shape[1]
    slots_all = expert_count * capacity
    placing = placement(targets(expert_of, expert_count, capacity, 0), slots_all)
    packed = dot(placing, tokens, MATMUL).astype(BF16)
    arrived = lax.all_to_all(
        packed.reshape(expert_count, capacity, feature_width), "exp", 0, 0, tiled=True
    )
    rows = arrived.reshape(slots_all, feature_width)
    gate_act, up_act = dot(rows, w_gate[0], LAST), dot(rows, w_up[0], LAST)
    cotan = d_hidden.reshape(slots_all, w_gate.shape[1])
    sigma, d_gate, d_up = gradients(gate_act, up_act, cotan)
    hidden = (gate_act * sigma * up_act).astype(BF16)

    def reduced(d_act):
        total = lax.psum(dot(d_act, rows, FIRST).astype(BF16), "rep").astype(F32)
        return (total * (1.0 / replica_count)).astype(BF16)[None]

    term = dot(d_gate, w_gate[0], MATMUL) + dot(d_up, w_up[0], MATMUL)
    outgoing = term.astype(BF16).reshape(expert_count, capacity, feature_width)
    returned = lax.all_to_all(outgoing, "exp", 0, 0, tiled=True)
    unpacked = dot(placing, returned.reshape(slots_all, feature_width), FIRST)
    d_tokens = lax.psum_scatter(unpacked.astype(BF16), "shard", scatter_dimension=1, tiled=True)
    return hidden.reshape(d_hidden.shape), d_tokens, reduced(d_gate), reduced(d_up)


def across(x, axis, bit):
    size = lax.axis_size(axis)
    return lax.ppermute(x, axis, [(i, i ^ bit) for i in range(size)])


def turned(x, axis, step):
    size = lax.axis_size(axis)
    return lax.ppermute(x, axis, [(i, (i + step) % size) for i in range(size)])


VMEM = pl.BlockSpec(memory_space=pltpu.VMEM)
ANY = pl.BlockSpec(memory_space=pl.ANY)
HBM = pl.BlockSpec(memory_space=pltpu.HBM)


def call(kernel, ins, outs, args, scratch=(), name=None, limit=24, flops=1, out_spec=VMEM):
    return pl.pallas_call(
        kernel,
        in_specs=ins,
        out_specs=[out_spec] * len(outs),
        out_shape=outs,
        scratch_shapes=list(scratch),
        compiler_params=pltpu.CompilerParams(vmem_limit_bytes=limit << 20),
        cost_estimate=pl.CostEstimate(flops=flops, transcendentals=0, bytes_accessed=1),
        name=name,
    )(*args)


def like(*shape, dtype=BF16):
    return jax.ShapeDtypeStruct(shape, dtype)


def after(values, *earlier):
    held = lax.optimization_barrier((tuple(values), earlier))
    return list(held[0])


def place_rows(expert_ref, capacity):
    count, first = lax.axis_size("exp"), lax.axis_index("exp")
    tokens = expert_ref.shape[1]
    routed = jnp.broadcast_to(expert_ref[...], (tokens, tokens))
    rows = lax.broadcasted_iota(jnp.int32, (tokens, tokens), 0)
    columns = lax.broadcasted_iota(jnp.int32, (tokens, tokens), 1)
    chosen = routed == rows
    before = dot(chosen.astype(BF16), (rows < columns).astype(BF16), MATMUL)
    slot = jnp.sum(jnp.where(chosen, before, 0.0), axis=0, keepdims=True).astype(jnp.int32)
    turn = routed[:1] - first
    target = jnp.where(turn < 0, turn + count, turn) * capacity + slot
    slots = lax.broadcasted_iota(jnp.int32, (count * capacity, tokens), 0)
    return (slots == target).astype(BF16)


def side_of(core, half):
    return pl.ds(pl.multiple_of(core * half, 128), half)


def load_kernel(gate_ref, up_ref, out, sem):
    core, (units, width) = lax.axis_index("shard"), gate_ref.shape
    half, copies = width // 2, []
    for i, ref in enumerate((gate_ref, up_ref)):
        for j, side in enumerate((core, 1 - core)):
            to = out.at[i * units : (i + 1) * units, j * half : (j + 1) * half]
            copies.append(pltpu.make_async_copy(ref.at[:, side_of(side, half)], to, sem.at[i, j]))
    for c in copies:
        c.start()
    for c in copies:
        c.wait()


def pack_kernel(capacity, expert_hbm, tokens_hbm, *refs):
    *outs, experts, mine, theirs, sem = refs
    count, core = lax.axis_size("exp"), lax.axis_index("shard")
    half = mine.shape[1]
    first = pltpu.make_async_copy(expert_hbm, experts, sem.at[0])
    second = pltpu.make_async_copy(tokens_hbm.at[:, side_of(core, half)], mine, sem.at[1])
    third = pltpu.make_async_copy(tokens_hbm.at[:, side_of(1 - core, half)], theirs, sem.at[2])
    first.start()
    second.start()
    third.start()
    first.wait()
    placing = place_rows(experts, capacity)
    second.wait()
    packed = dot(placing, mine[...], MATMUL).astype(BF16)
    for k in range(count):
        outs[k][...] = packed[k * capacity : (k + 1) * capacity]
    third.wait()
    outs[count][...] = dot(placing[:capacity], theirs[...], MATMUL).astype(BF16)


def place_kernel(capacity, expert_ref, out):
    out[...] = jnp.transpose(place_rows(expert_ref, capacity))


def unpack_kernel(placing_ref, *refs):
    *pieces, out = refs
    rows = jnp.concatenate([p[...] for p in pieces])
    out[...] = dot(placing_ref[...], rows, MATMUL).astype(BF16)


def sum_kernel(kept_ref, *refs):
    got_ref, *outs = refs
    capacity = outs[0].shape[0]
    for k, out in enumerate(outs):
        at = pl.ds(k * capacity, capacity)
        out[...] = (kept_ref[at].astype(F32) + got_ref[at].astype(F32)).astype(BF16)


def joined(refs, columns=slice(None)):
    return jnp.concatenate([r[:, columns] for r in refs])


def activations(pieces, others, rows_ref):
    half = rows_ref.shape[1] // 2
    acts = dot(joined(pieces), rows_ref[:, :half], LAST)
    return acts + dot(joined(others), rows_ref[:, half:], LAST)


def source_of(k):
    count = lax.axis_size("exp")
    return lax.rem(lax.axis_index("exp") - k + count, count)


def own_kernel(blocks, *refs):
    n = len(blocks)
    pieces, others = refs[:n], refs[n : 2 * n]
    cotan_ref, rows_ref, d_ref, sent_ref, hidden_ref = refs[2 * n :]
    capacity, units = cotan_ref.shape[1:]
    acts = activations(pieces, others, rows_ref)
    for i, k in enumerate(blocks):
        at = slice(i * capacity, (i + 1) * capacity)
        gate, up = acts[at, :units], acts[at, units:]
        sigma, d_gate, d_up = gradients(gate, up, cotan_ref[source_of(k)])
        hidden_ref[source_of(k)] = (gate * sigma * up).astype(BF16)
        d_ref[at, :units] = d_gate
        d_ref[at, units:] = d_up
    sent_ref[...] = dot(d_ref[...], rows_ref[:, sent_ref.shape[1] :], MATMUL).astype(BF16)


def kept_kernel(d_ref, rows_ref, kept_ref):
    mine = rows_ref[:, : kept_ref.shape[1]]
    kept_ref[...] = dot(d_ref[...], mine, MATMUL).astype(BF16)


def part_kernel(plan, n, *refs):
    pieces, others = refs[:n], refs[n : 2 * n]
    near, far, rows_ref, d_ref = refs[2 * n :]
    capacity, units = near.shape[1:]
    acts = activations(pieces, others, rows_ref)
    for i, (k, group) in enumerate(plan):
        at = slice(i * capacity, (i + 1) * capacity)
        source = source_of(k)
        cotan = near[source] if group == 2 else far[0 if group == 1 else 1, source]
        _, d_gate, d_up = gradients(acts[at, :units], acts[at, units:], cotan)
        d_ref[at, :units] = d_gate
        d_ref[at, units:] = d_up


def hold(ds, held):
    start = 0
    for d in ds:
        held[start : start + d.shape[0]] = d[...]
        start += d.shape[0]


def grad_kernel(n, *refs):
    pieces, others = refs[:n], refs[n : 2 * n]
    *ds, out, held = refs[2 * n :]
    hold(ds, held)
    half = out.shape[1] // 2
    for j, rows in enumerate((pieces, others)):
        out[:, j * half : (j + 1) * half] = dot(held[...], joined(rows), FIRST)


def last_grad_kernel(scale, n, *refs):
    pieces, others = refs[:n], refs[n : 2 * n]
    *ds, earlier, gate_out, up_out, staged, held, sem = refs[2 * n :]
    hold(ds, held)
    core, units, half = lax.axis_index("shard"), gate_out.shape[0], staged.shape[1] // 2
    wide, copies = half // 5, []
    for j, (rows, side) in enumerate(((pieces, core), (others, 1 - core))):
        for i, (start, stop) in enumerate(((0, 2), (2, 4), (4, 5))):
            columns = slice(start * wide, stop * wide)
            at = slice(j * half + start * wide, j * half + stop * wide)
            total = dot(held[...], joined(rows, columns), FIRST)
            staged[:, at] = ((total + earlier[:, at]) * scale).astype(BF16)
            to = pl.ds(pl.multiple_of(side * half + start * wide, 128), (stop - start) * wide)
            for h, out in enumerate((gate_out, up_out)):
                copies.append(
                    pltpu.make_async_copy(
                        staged.at[h * units : (h + 1) * units, at], out.at[:, to], sem.at[j, i, h]
                    )
                )
                copies[-1].start()
    for c in copies:
        c.wait()


def swap(x):
    return across(x, "shard", 1)


def gather_plan(tokens, expert_of, w_gate, w_up, d_hidden):
    count = lax.axis_size("exp")
    capacity = d_hidden.shape[3]
    width = tokens.shape[1]
    half = width // 2
    hidden_width = w_gate.shape[1]
    gate_rows, up_rows, cotan = w_gate[0], w_up[0], d_hidden[0, 0]
    experts = expert_of.reshape(1, -1)
    piece = like(capacity, half)

    def own(pair, rows, others):
        n = len(pair) * capacity
        return call(
            functools.partial(own_kernel, pair),
            [VMEM] * (2 * len(rows) + 2),
            [like(n, 2 * hidden_width), like(n, half), like(len(pair), capacity, hidden_width)],
            [*rows, *others, cotan, both_rows],
            name="own",
        )

    def part(plan, pieces, others, near, far):
        n = sum(p.shape[0] for p in pieces)
        (d,) = call(
            functools.partial(part_kernel, plan, len(pieces)),
            [VMEM] * (2 * len(pieces) + 3),
            [like(n, 2 * hidden_width)],
            [*pieces, *others, near, far, both_rows],
            name="part",
        )
        return d

    def add(kept, got):
        return call(sum_kernel, [VMEM] * 2, [piece] * count, [kept, got], name="sum")

    *blocks, other = call(
        functools.partial(pack_kernel, capacity),
        [HBM, HBM],
        [piece] * (count + 1),
        [pltpu.with_memory_space_constraint(x, pltpu.HBM) for x in (experts, tokens)],
        scratch=[
            pltpu.VMEM(experts.shape, jnp.int32),
            pltpu.VMEM((tokens.shape[0], half), BF16),
            pltpu.VMEM((tokens.shape[0], half), BF16),
            pltpu.SemaphoreType.DMA((3,)),
        ],
        name="pack",
    )
    c0 = blocks[0]
    z1, z2, z3 = (turned(blocks[k], "exp", k) for k in (1, 2, 3))
    (cotan_sent,) = after([cotan], c0)
    c0_near = across(c0, "rep", 1)
    cotan_near = across(cotan_sent, "rep", 2)
    (both_rows,) = call(
        load_kernel,
        [HBM] * 2,
        [like(2 * hidden_width, width)],
        after([pltpu.with_memory_space_constraint(x, pltpu.HBM) for x in (gate_rows, up_rows)], c0),
        scratch=[pltpu.SemaphoreType.DMA((2, 2))],
        name="load",
    )
    c0_kept, c0_near_kept = after([c0, c0_near], both_rows)
    c0_both = jnp.concatenate([c0_kept, c0_near_kept])
    cotan_both = jnp.stack([cotan, cotan_near])
    c0_far = across(c0_both, "rep", 2)
    cotan_far = across(cotan_both, "rep", 1)

    z1, z2, z3 = after([z1, z2, z3], c0_both, cotan_both)
    o1, o2, o3 = swap(z1), swap(z2), swap(z3)
    c123 = jnp.concatenate([z1, z2, z3])
    o1, o2, o3 = after([o1, o2, o3], c0_far, cotan_far)
    d_a, sent, hidden = own((0, 1, 2, 3), [c0, z1, z2, z3], [other, o1, o2, o3])
    (kept,) = call(
        kept_kernel, [VMEM] * 2, [like(count * capacity, half)], [d_a, both_rows], name="kept"
    )
    c123_sent, c0_near_sent, c0_far_sent = after([c123, c0_near, c0_far], sent)
    c123_x, c123_y = across(c123_sent, "rep", 1), across(c123_sent, "rep", 2)
    c0_others = [swap(c0_near_sent), swap(c0_far_sent)]
    r0, r1, r2, r3 = add(kept, swap(sent))
    r1, r2, r3 = turned(r1, "exp", -1), turned(r2, "exp", -2), turned(r3, "exp", -3)

    plan = ((0, 1), (0, 2), (0, 3))
    d_c = part(plan, [c0_near, c0_far], c0_others, cotan_near, cotan_far)
    (total,) = call(
        functools.partial(grad_kernel, 6),
        [VMEM] * 14,
        [like(2 * hidden_width, width, dtype=F32)],
        [c0, z1, z2, z3, c0_near, c0_far, other, o1, o2, o3, *c0_others, d_a, d_c],
        scratch=[pltpu.VMEM((d_a.shape[0] + d_c.shape[0], 2 * hidden_width), BF16)],
        name="grads_near",
        limit=32,
    )
    (placing,) = call(
        functools.partial(place_kernel, capacity),
        [VMEM],
        [like(tokens.shape[0], count * capacity)],
        after([experts], d_c),
        name="place",
    )
    c123_x, c123_y = after([c123_x, c123_y], total, placing)
    cut = (c123.shape[0] // 2 + 15) // 16 * 16
    far_sent = [across(c123_x[:cut], "rep", 2), across(c123_y[cut:], "rep", 1)]
    (d_tokens,) = call(
        unpack_kernel,
        [VMEM] * (1 + count),
        [like(tokens.shape[0], half)],
        [placing, r0, r1, r2, r3],
        name="unpack",
        flops=6*10**9,
    )
    (c123_x,), (c123_y,) = after([c123_x], r1), after([c123_y], r2)
    far_sent = after(far_sent, d_tokens)
    plan = tuple((k, group) for group in (1, 2) for k in (1, 2, 3))
    pieces, others = [c123_x, c123_y], [swap(c123_x), swap(c123_y)]
    d_d = part(plan, pieces, others, cotan_near, cotan_far)
    plan = tuple((k, 3) for k in (1, 2, 3))
    far_others = after([swap(f) for f in far_sent], d_d)
    d_e = part(plan, far_sent, far_others, cotan_near, cotan_far)
    grad_gate, grad_up = call(
        functools.partial(last_grad_kernel, 1.0 / lax.axis_size("rep"), 4),
        [VMEM] * 11,
        [like(hidden_width, width)] * 2,
        [*pieces, *far_sent, *others, *far_others, d_d, d_e, total],
        scratch=[
            pltpu.VMEM((2 * hidden_width, width), BF16),
            pltpu.VMEM((d_d.shape[0] + d_e.shape[0], 2 * hidden_width), BF16),
            pltpu.SemaphoreType.DMA((2, 3, 2)),
        ],
        name="grads",
        limit=32,
        out_spec=HBM,
    )
    return hidden.reshape(d_hidden.shape), d_tokens, grad_gate[None], grad_up[None]


def local(tokens, expert_of, w_gate, w_up, d_hidden):
    replica_count, shard_count = lax.axis_size("rep"), lax.axis_size("shard")
    slots_all = d_hidden.shape[2] * d_hidden.shape[3]
    hidden_width, feature_width = w_gate.shape[1:]
    gathered = slots_all * (feature_width // shard_count + hidden_width) * replica_count
    reduced = 4 * hidden_width * feature_width
    if replica_count == 4 and shard_count == 2 and lax.axis_size("exp") == 4 and gathered < reduced:
        return gather_plan(tokens, expert_of, w_gate, w_up, d_hidden)
    return reduce_plan(tokens, expert_of, w_gate, w_up, d_hidden)


def solution(mesh):
    in_specs = (
        P(("rep", "exp"), None),
        P(("rep", "exp"), None),
        P("exp", "shard", None),
        P("exp", "shard", None),
        P("rep", "exp", None, None, "shard"),
    )
    out_specs = (
        P("rep", "exp", None, None, "shard"),
        P(("rep", "exp"), "shard"),
        P("exp", "shard", None),
        P("exp", "shard", None),
    )
    return jax.shard_map(local, mesh=mesh, in_specs=in_specs, out_specs=out_specs, check_vma=False)
```

```python
import functools

import jax
import jax.numpy as jnp
from jax import lax
from jax.experimental import pallas as pl
from jax.experimental.pallas import tpu as pltpu
from jax.sharding import PartitionSpec as P

BF16 = jnp.bfloat16
F32 = jnp.float32
LAST = (((1,), (1,)), ((), ()))
FIRST = (((0,), (0,)), ((), ()))
MATMUL = (((1,), (0,)), ((), ()))


def dot(a, b, dims):
    return lax.dot_general(a, b, dims, preferred_element_type=F32)


def targets(expert_of, expert_count, capacity, first):
    routed = expert_of[:, 0]
    chosen = (routed[:, None] == jnp.arange(expert_count, dtype=jnp.int32)[None, :]).astype(
        jnp.int32
    )
    slot_index = jnp.sum(chosen * (jnp.cumsum(chosen, axis=0) - 1), axis=1)
    return lax.rem(routed - first + expert_count, expert_count) * capacity + slot_index


def placement(target, slots_all):
    return (jnp.arange(slots_all, dtype=jnp.int32)[:, None] == target[None, :]).astype(BF16)


def gradients(gate_act, up_act, cotan):
    sigma = jax.nn.sigmoid(gate_act)
    cotan = cotan.astype(F32)
    d_gate = (cotan * up_act * sigma * (1.0 + gate_act * (1.0 - sigma))).astype(BF16)
    d_up = (cotan * gate_act * sigma).astype(BF16)
    return sigma, d_gate, d_up


def reduce_plan(tokens, expert_of, w_gate, w_up, d_hidden):
    expert_count = lax.axis_size("exp")
    replica_count = lax.axis_size("rep")
    capacity = d_hidden.shape[3]
    feature_width = tokens.shape[1]
    slots_all = expert_count * capacity
    placing = placement(targets(expert_of, expert_count, capacity, 0), slots_all)
    packed = dot(placing, tokens, MATMUL).astype(BF16)
    arrived = lax.all_to_all(
        packed.reshape(expert_count, capacity, feature_width), "exp", 0, 0, tiled=True
    )
    rows = arrived.reshape(slots_all, feature_width)
    gate_act, up_act = dot(rows, w_gate[0], LAST), dot(rows, w_up[0], LAST)
    cotan = d_hidden.reshape(slots_all, w_gate.shape[1])
    sigma, d_gate, d_up = gradients(gate_act, up_act, cotan)
    hidden = (gate_act * sigma * up_act).astype(BF16)

    def reduced(d_act):
        total = lax.psum(dot(d_act, rows, FIRST).astype(BF16), "rep").astype(F32)
        return (total * (1.0 / replica_count)).astype(BF16)[None]

    term = dot(d_gate, w_gate[0], MATMUL) + dot(d_up, w_up[0], MATMUL)
    outgoing = term.astype(BF16).reshape(expert_count, capacity, feature_width)
    returned = lax.all_to_all(outgoing, "exp", 0, 0, tiled=True)
    unpacked = dot(placing, returned.reshape(slots_all, feature_width), FIRST)
    d_tokens = lax.psum_scatter(unpacked.astype(BF16), "shard", scatter_dimension=1, tiled=True)
    return hidden.reshape(d_hidden.shape), d_tokens, reduced(d_gate), reduced(d_up)


def across(x, axis, bit):
    size = lax.axis_size(axis)
    return lax.ppermute(x, axis, [(i, i ^ bit) for i in range(size)])


def turned(x, axis, step):
    size = lax.axis_size(axis)
    return lax.ppermute(x, axis, [(i, (i + step) % size) for i in range(size)])


VMEM = pl.BlockSpec(memory_space=pltpu.VMEM)
ANY = pl.BlockSpec(memory_space=pl.ANY)
HBM = pl.BlockSpec(memory_space=pltpu.HBM)


def call(kernel, ins, outs, args, scratch=(), name=None, limit=24, flops=1, out_spec=VMEM):
    return pl.pallas_call(
        kernel,
        in_specs=ins,
        out_specs=[out_spec] * len(outs),
        out_shape=outs,
        scratch_shapes=list(scratch),
        compiler_params=pltpu.CompilerParams(vmem_limit_bytes=limit << 20),
        cost_estimate=pl.CostEstimate(flops=flops, transcendentals=0, bytes_accessed=1),
        name=name,
    )(*args)


def like(*shape, dtype=BF16):
    return jax.ShapeDtypeStruct(shape, dtype)


def after(values, *earlier):
    held = lax.optimization_barrier((tuple(values), earlier))
    return list(held[0])


def place_rows(expert_ref, capacity):
    count, first = lax.axis_size("exp"), lax.axis_index("exp")
    tokens = expert_ref.shape[1]
    routed = jnp.broadcast_to(expert_ref[...], (tokens, tokens))
    rows = lax.broadcasted_iota(jnp.int32, (tokens, tokens), 0)
    columns = lax.broadcasted_iota(jnp.int32, (tokens, tokens), 1)
    chosen = routed == rows
    before = dot(chosen.astype(BF16), (rows < columns).astype(BF16), MATMUL)
    slot = jnp.sum(jnp.where(chosen, before, 0.0), axis=0, keepdims=True).astype(jnp.int32)
    turn = routed[:1] - first
    target = jnp.where(turn < 0, turn + count, turn) * capacity + slot
    slots = lax.broadcasted_iota(jnp.int32, (count * capacity, tokens), 0)
    return (slots == target).astype(BF16)


def side_of(core, half):
    return pl.ds(pl.multiple_of(core * half, 128), half)


def load_kernel(gate_ref, up_ref, out, sem):
    core, (units, width) = lax.axis_index("shard"), gate_ref.shape
    half, copies = width // 2, []
    for i, ref in enumerate((gate_ref, up_ref)):
        for j, side in enumerate((core, 1 - core)):
            to = out.at[i * units : (i + 1) * units, j * half : (j + 1) * half]
            copies.append(pltpu.make_async_copy(ref.at[:, side_of(side, half)], to, sem.at[i, j]))
    for c in copies:
        c.start()
    for c in copies:
        c.wait()


def pack_kernel(capacity, expert_hbm, tokens_hbm, *refs):
    *outs, experts, mine, theirs, sem = refs
    count, core = lax.axis_size("exp"), lax.axis_index("shard")
    half = mine.shape[1]
    first = pltpu.make_async_copy(expert_hbm, experts, sem.at[0])
    second = pltpu.make_async_copy(tokens_hbm.at[:, side_of(core, half)], mine, sem.at[1])
    third = pltpu.make_async_copy(tokens_hbm.at[:, side_of(1 - core, half)], theirs, sem.at[2])
    first.start()
    second.start()
    third.start()
    first.wait()
    placing = place_rows(experts, capacity)
    second.wait()
    packed = dot(placing, mine[...], MATMUL).astype(BF16)
    for k in range(count):
        outs[k][...] = packed[k * capacity : (k + 1) * capacity]
    third.wait()
    outs[count][...] = dot(placing[:capacity], theirs[...], MATMUL).astype(BF16)


def place_kernel(capacity, expert_ref, out):
    out[...] = jnp.transpose(place_rows(expert_ref, capacity))


def unpack_kernel(placing_ref, *refs):
    *pieces, out = refs
    rows = jnp.concatenate([p[...] for p in pieces])
    out[...] = dot(placing_ref[...], rows, MATMUL).astype(BF16)


def sum_kernel(kept_ref, *refs):
    got_ref, *outs = refs
    capacity = outs[0].shape[0]
    for k, out in enumerate(outs):
        at = pl.ds(k * capacity, capacity)
        out[...] = (kept_ref[at].astype(F32) + got_ref[at].astype(F32)).astype(BF16)


def joined(refs, columns=slice(None)):
    return jnp.concatenate([r[:, columns] for r in refs])


def activations(pieces, others, rows_ref):
    half = rows_ref.shape[1] // 2
    acts = dot(joined(pieces), rows_ref[:, :half], LAST)
    return acts + dot(joined(others), rows_ref[:, half:], LAST)


def source_of(k):
    count = lax.axis_size("exp")
    return lax.rem(lax.axis_index("exp") - k + count, count)


def own_kernel(blocks, *refs):
    n = len(blocks)
    pieces, others = refs[:n], refs[n : 2 * n]
    cotan_ref, rows_ref, d_ref, sent_ref, hidden_ref = refs[2 * n :]
    capacity, units = cotan_ref.shape[1:]
    acts = activations(pieces, others, rows_ref)
    for i, k in enumerate(blocks):
        at = slice(i * capacity, (i + 1) * capacity)
        gate, up = acts[at, :units], acts[at, units:]
        sigma, d_gate, d_up = gradients(gate, up, cotan_ref[source_of(k)])
        hidden_ref[source_of(k)] = (gate * sigma * up).astype(BF16)
        d_ref[at, :units] = d_gate
        d_ref[at, units:] = d_up
    sent_ref[...] = dot(d_ref[...], rows_ref[:, sent_ref.shape[1] :], MATMUL).astype(BF16)


def kept_kernel(d_ref, rows_ref, kept_ref):
    mine = rows_ref[:, : kept_ref.shape[1]]
    kept_ref[...] = dot(d_ref[...], mine, MATMUL).astype(BF16)


def part_kernel(plan, n, *refs):
    pieces, others = refs[:n], refs[n : 2 * n]
    near, far, rows_ref, *begun, d_ref = refs[2 * n :]
    capacity, units = near.shape[1:]
    if begun:
        half = rows_ref.shape[1] // 2
        acts = begun[0][...] + dot(joined(others), rows_ref[:, half:], LAST)
    else:
        acts = activations(pieces, others, rows_ref)
    for i, (k, group) in enumerate(plan):
        at = slice(i * capacity, (i + 1) * capacity)
        source = source_of(k)
        cotan = near[source] if group == 2 else far[0 if group == 1 else 1, source]
        _, d_gate, d_up = gradients(acts[at, :units], acts[at, units:], cotan)
        d_ref[at, :units] = d_gate
        d_ref[at, units:] = d_up


def begin_kernel(*refs):
    *pieces, rows_ref, out = refs
    out[...] = dot(joined(pieces), rows_ref[:, : rows_ref.shape[1] // 2], LAST)


def hold(ds, held):
    start = 0
    for d in ds:
        held[start : start + d.shape[0]] = d[...]
        start += d.shape[0]


def grad_kernel(n, *refs):
    pieces, others = refs[:n], refs[n : 2 * n]
    *ds, out, held = refs[2 * n :]
    hold(ds, held)
    half = out.shape[1] // 2
    for j, rows in enumerate((pieces, others)):
        out[:, j * half : (j + 1) * half] = dot(held[...], joined(rows), FIRST)


def last_grad_kernel(scale, n, *refs):
    pieces, others = refs[:n], refs[n : 2 * n]
    *ds, earlier, gate_out, up_out, staged, held, sem = refs[2 * n :]
    hold(ds, held)
    core, units, half = lax.axis_index("shard"), gate_out.shape[0], staged.shape[1] // 2
    wide, copies = half // 5, []
    for j, (rows, side) in enumerate(((pieces, core), (others, 1 - core))):
        for i, (start, stop) in enumerate(((0, 2), (2, 4), (4, 5))):
            columns = slice(start * wide, stop * wide)
            at = slice(j * half + start * wide, j * half + stop * wide)
            total = dot(held[...], joined(rows, columns), FIRST)
            staged[:, at] = ((total + earlier[:, at]) * scale).astype(BF16)
            to = pl.ds(pl.multiple_of(side * half + start * wide, 128), (stop - start) * wide)
            for h, out in enumerate((gate_out, up_out)):
                copies.append(
                    pltpu.make_async_copy(
                        staged.at[h * units : (h + 1) * units, at], out.at[:, to], sem.at[j, i, h]
                    )
                )
                copies[-1].start()
    for c in copies:
        c.wait()


def swap(x):
    return across(x, "shard", 1)


def gather_plan(tokens, expert_of, w_gate, w_up, d_hidden):
    count = lax.axis_size("exp")
    capacity = d_hidden.shape[3]
    width = tokens.shape[1]
    half = width // 2
    hidden_width = w_gate.shape[1]
    gate_rows, up_rows, cotan = w_gate[0], w_up[0], d_hidden[0, 0]
    experts = expert_of.reshape(1, -1)
    piece = like(capacity, half)

    def own(pair, rows, others):
        n = len(pair) * capacity
        return call(
            functools.partial(own_kernel, pair),
            [VMEM] * (2 * len(rows) + 2),
            [like(n, 2 * hidden_width), like(n, half), like(len(pair), capacity, hidden_width)],
            [*rows, *others, cotan, both_rows],
            name="own",
        )

    def part(plan, pieces, others, near, far, begun=()):
        n = sum(p.shape[0] for p in pieces)
        (d,) = call(
            functools.partial(part_kernel, plan, len(pieces)),
            [VMEM] * (2 * len(pieces) + 3 + len(begun)),
            [like(n, 2 * hidden_width)],
            [*pieces, *others, near, far, both_rows, *begun],
            name="part",
        )
        return d

    def add(kept, got):
        return call(sum_kernel, [VMEM] * 2, [piece] * count, [kept, got], name="sum")

    *blocks, other = call(
        functools.partial(pack_kernel, capacity),
        [HBM, HBM],
        [piece] * (count + 1),
        [pltpu.with_memory_space_constraint(x, pltpu.HBM) for x in (experts, tokens)],
        scratch=[
            pltpu.VMEM(experts.shape, jnp.int32),
            pltpu.VMEM((tokens.shape[0], half), BF16),
            pltpu.VMEM((tokens.shape[0], half), BF16),
            pltpu.SemaphoreType.DMA((3,)),
        ],
        name="pack",
    )
    c0 = blocks[0]
    z1, z2, z3 = (turned(blocks[k], "exp", k) for k in (1, 2, 3))
    (cotan_sent,) = after([cotan], c0)
    c0_near = across(c0, "rep", 1)
    cotan_near = across(cotan_sent, "rep", 2)
    (both_rows,) = call(
        load_kernel,
        [HBM] * 2,
        [like(2 * hidden_width, width)],
        after([pltpu.with_memory_space_constraint(x, pltpu.HBM) for x in (gate_rows, up_rows)], c0),
        scratch=[pltpu.SemaphoreType.DMA((2, 2))],
        name="load",
    )
    c0_kept, c0_near_kept = after([c0, c0_near], both_rows)
    c0_both = jnp.concatenate([c0_kept, c0_near_kept])
    cotan_both = jnp.stack([cotan, cotan_near])
    c0_far = across(c0_both, "rep", 2)
    cotan_far = across(cotan_both, "rep", 1)

    z1, z2, z3 = after([z1, z2, z3], c0_both, cotan_both)
    o1, o2, o3 = swap(z1), swap(z2), swap(z3)
    c123 = jnp.concatenate([z1, z2, z3])
    o1, o2, o3 = after([o1, o2, o3], c0_far, cotan_far)
    d_a, sent, hidden = own((0, 1, 2, 3), [c0, z1, z2, z3], [other, o1, o2, o3])
    (kept,) = call(
        kept_kernel, [VMEM] * 2, [like(count * capacity, half)], [d_a, both_rows], name="kept"
    )
    c123_sent, c0_near_sent, c0_far_sent = after([c123, c0_near, c0_far], sent)
    c123_x, c123_y = across(c123_sent, "rep", 1), across(c123_sent, "rep", 2)
    c0_others = [swap(c0_near_sent), swap(c0_far_sent)]
    r0, r1, r2, r3 = add(kept, swap(sent))
    r1, r2, r3 = turned(r1, "exp", -1), turned(r2, "exp", -2), turned(r3, "exp", -3)

    plan = ((0, 1), (0, 2), (0, 3))
    d_c = part(plan, [c0_near, c0_far], c0_others, cotan_near, cotan_far)
    (total,) = call(
        functools.partial(grad_kernel, 6),
        [VMEM] * 14,
        [like(2 * hidden_width, width, dtype=F32)],
        [c0, z1, z2, z3, c0_near, c0_far, other, o1, o2, o3, *c0_others, d_a, d_c],
        scratch=[pltpu.VMEM((d_a.shape[0] + d_c.shape[0], 2 * hidden_width), BF16)],
        name="grads_near",
        limit=32,
    )
    (placing,) = call(
        functools.partial(place_kernel, capacity),
        [VMEM],
        [like(tokens.shape[0], count * capacity)],
        after([experts], d_c),
        name="place",
    )
    c123_x, c123_y = after([c123_x, c123_y], total, placing)
    cut = (c123.shape[0] // 2 + 15) // 16 * 16
    far_sent = [across(c123_x[:cut], "rep", 2), across(c123_y[cut:], "rep", 1)]
    (c123_x,), (c123_y,) = after([c123_x], r1), after([c123_y], r2)
    (begun,) = call(
        begin_kernel,
        [VMEM] * 3,
        [like(2 * c123.shape[0], 2 * hidden_width, dtype=F32)],
        [c123_x, c123_y, both_rows],
        name="begin",
    )
    (r3,) = after([r3], begun)
    (d_tokens,) = call(
        unpack_kernel,
        [VMEM] * (1 + count),
        [like(tokens.shape[0], half)],
        [placing, r0, r1, r2, r3],
        name="unpack",
        flops=6*10**9,
    )
    far_sent = after(far_sent, d_tokens)
    plan = tuple((k, group) for group in (1, 2) for k in (1, 2, 3))
    pieces, others = [c123_x, c123_y], [swap(c123_x), swap(c123_y)]
    d_d = part(plan, pieces, others, cotan_near, cotan_far, [begun])
    plan = tuple((k, 3) for k in (1, 2, 3))
    far_others = after([swap(f) for f in far_sent], d_d)
    d_e = part(plan, far_sent, far_others, cotan_near, cotan_far)
    grad_gate, grad_up = call(
        functools.partial(last_grad_kernel, 1.0 / lax.axis_size("rep"), 4),
        [VMEM] * 11,
        [like(hidden_width, width)] * 2,
        [*pieces, *far_sent, *others, *far_others, d_d, d_e, total],
        scratch=[
            pltpu.VMEM((2 * hidden_width, width), BF16),
            pltpu.VMEM((d_d.shape[0] + d_e.shape[0], 2 * hidden_width), BF16),
            pltpu.SemaphoreType.DMA((2, 3, 2)),
        ],
        name="grads",
        limit=32,
        out_spec=HBM,
    )
    return hidden.reshape(d_hidden.shape), d_tokens, grad_gate[None], grad_up[None]


def local(tokens, expert_of, w_gate, w_up, d_hidden):
    replica_count, shard_count = lax.axis_size("rep"), lax.axis_size("shard")
    slots_all = d_hidden.shape[2] * d_hidden.shape[3]
    hidden_width, feature_width = w_gate.shape[1:]
    gathered = slots_all * (feature_width // shard_count + hidden_width) * replica_count
    reduced = 4 * hidden_width * feature_width
    if replica_count == 4 and shard_count == 2 and lax.axis_size("exp") == 4 and gathered < reduced:
        return gather_plan(tokens, expert_of, w_gate, w_up, d_hidden)
    return reduce_plan(tokens, expert_of, w_gate, w_up, d_hidden)


def solution(mesh):
    in_specs = (
        P(("rep", "exp"), None),
        P(("rep", "exp"), None),
        P("exp", "shard", None),
        P("exp", "shard", None),
        P("rep", "exp", None, None, "shard"),
    )
    out_specs = (
        P("rep", "exp", None, None, "shard"),
        P(("rep", "exp"), "shard"),
        P("exp", "shard", None),
        P("exp", "shard", None),
    )
    return jax.shard_map(local, mesh=mesh, in_specs=in_specs, out_specs=out_specs, check_vma=False)
```

```python
import functools

import jax
import jax.numpy as jnp
from jax import lax
from jax.experimental import pallas as pl
from jax.experimental.pallas import tpu as pltpu
from jax.sharding import PartitionSpec as P

BF16 = jnp.bfloat16
F32 = jnp.float32
LAST = (((1,), (1,)), ((), ()))
FIRST = (((0,), (0,)), ((), ()))
MATMUL = (((1,), (0,)), ((), ()))


def dot(a, b, dims):
    return lax.dot_general(a, b, dims, preferred_element_type=F32)


def targets(expert_of, expert_count, capacity, first):
    routed = expert_of[:, 0]
    chosen = (routed[:, None] == jnp.arange(expert_count, dtype=jnp.int32)[None, :]).astype(
        jnp.int32
    )
    slot_index = jnp.sum(chosen * (jnp.cumsum(chosen, axis=0) - 1), axis=1)
    return lax.rem(routed - first + expert_count, expert_count) * capacity + slot_index


def placement(target, slots_all):
    return (jnp.arange(slots_all, dtype=jnp.int32)[:, None] == target[None, :]).astype(BF16)


def gradients(gate_act, up_act, cotan):
    sigma = jax.nn.sigmoid(gate_act)
    cotan = cotan.astype(F32)
    d_gate = (cotan * up_act * sigma * (1.0 + gate_act * (1.0 - sigma))).astype(BF16)
    d_up = (cotan * gate_act * sigma).astype(BF16)
    return sigma, d_gate, d_up


def reduce_plan(tokens, expert_of, w_gate, w_up, d_hidden):
    expert_count = lax.axis_size("exp")
    replica_count = lax.axis_size("rep")
    capacity = d_hidden.shape[3]
    feature_width = tokens.shape[1]
    slots_all = expert_count * capacity
    placing = placement(targets(expert_of, expert_count, capacity, 0), slots_all)
    packed = dot(placing, tokens, MATMUL).astype(BF16)
    arrived = lax.all_to_all(
        packed.reshape(expert_count, capacity, feature_width), "exp", 0, 0, tiled=True
    )
    rows = arrived.reshape(slots_all, feature_width)
    gate_act, up_act = dot(rows, w_gate[0], LAST), dot(rows, w_up[0], LAST)
    cotan = d_hidden.reshape(slots_all, w_gate.shape[1])
    sigma, d_gate, d_up = gradients(gate_act, up_act, cotan)
    hidden = (gate_act * sigma * up_act).astype(BF16)

    def reduced(d_act):
        total = lax.psum(dot(d_act, rows, FIRST).astype(BF16), "rep").astype(F32)
        return (total * (1.0 / replica_count)).astype(BF16)[None]

    term = dot(d_gate, w_gate[0], MATMUL) + dot(d_up, w_up[0], MATMUL)
    outgoing = term.astype(BF16).reshape(expert_count, capacity, feature_width)
    returned = lax.all_to_all(outgoing, "exp", 0, 0, tiled=True)
    unpacked = dot(placing, returned.reshape(slots_all, feature_width), FIRST)
    d_tokens = lax.psum_scatter(unpacked.astype(BF16), "shard", scatter_dimension=1, tiled=True)
    return hidden.reshape(d_hidden.shape), d_tokens, reduced(d_gate), reduced(d_up)


def across(x, axis, bit):
    size = lax.axis_size(axis)
    return lax.ppermute(x, axis, [(i, i ^ bit) for i in range(size)])


def turned(x, axis, step):
    size = lax.axis_size(axis)
    return lax.ppermute(x, axis, [(i, (i + step) % size) for i in range(size)])


VMEM = pl.BlockSpec(memory_space=pltpu.VMEM)
ANY = pl.BlockSpec(memory_space=pl.ANY)
HBM = pl.BlockSpec(memory_space=pltpu.HBM)


def call(kernel, ins, outs, args, scratch=(), name=None, limit=24, flops=1, out_spec=VMEM):
    return pl.pallas_call(
        kernel,
        in_specs=ins,
        out_specs=[out_spec] * len(outs),
        out_shape=outs,
        scratch_shapes=list(scratch),
        compiler_params=pltpu.CompilerParams(vmem_limit_bytes=limit << 20),
        cost_estimate=pl.CostEstimate(flops=flops, transcendentals=0, bytes_accessed=1),
        name=name,
    )(*args)


def like(*shape, dtype=BF16):
    return jax.ShapeDtypeStruct(shape, dtype)


def after(values, *earlier):
    held = lax.optimization_barrier((tuple(values), earlier))
    return list(held[0])


def place_rows(expert_ref, capacity):
    count, first = lax.axis_size("exp"), lax.axis_index("exp")
    tokens = expert_ref.shape[1]
    routed = jnp.broadcast_to(expert_ref[...], (tokens, tokens))
    rows = lax.broadcasted_iota(jnp.int32, (tokens, tokens), 0)
    columns = lax.broadcasted_iota(jnp.int32, (tokens, tokens), 1)
    chosen = routed == rows
    before = dot(chosen.astype(BF16), (rows < columns).astype(BF16), MATMUL)
    slot = jnp.sum(jnp.where(chosen, before, 0.0), axis=0, keepdims=True).astype(jnp.int32)
    turn = routed[:1] - first
    target = jnp.where(turn < 0, turn + count, turn) * capacity + slot
    slots = lax.broadcasted_iota(jnp.int32, (count * capacity, tokens), 0)
    return (slots == target).astype(BF16)


def side_of(core, half):
    return pl.ds(pl.multiple_of(core * half, 128), half)


def load_kernel(capacity, gate_ref, up_ref, expert_hbm, tokens_hbm, out, other, *scratch):
    experts, theirs, sem, token_sem = scratch
    core, (units, width) = lax.axis_index("shard"), gate_ref.shape
    half, copies = width // 2, []
    for i, ref in enumerate((gate_ref, up_ref)):
        for j, side in enumerate((core, 1 - core)):
            to = out.at[i * units : (i + 1) * units, j * half : (j + 1) * half]
            copies.append(pltpu.make_async_copy(ref.at[:, side_of(side, half)], to, sem.at[i, j]))
    first = pltpu.make_async_copy(expert_hbm, experts, token_sem.at[0])
    second = pltpu.make_async_copy(tokens_hbm.at[:, side_of(1 - core, half)], theirs, token_sem.at[1])
    for c in (first, second, *copies):
        c.start()
    first.wait()
    placing = place_rows(experts, capacity)
    second.wait()
    other[...] = dot(placing[:capacity], theirs[...], MATMUL).astype(BF16)
    for c in copies:
        c.wait()


def pack_kernel(capacity, expert_hbm, tokens_hbm, *refs):
    *outs, experts, mine, sem = refs
    count, core = lax.axis_size("exp"), lax.axis_index("shard")
    half = mine.shape[1]
    first = pltpu.make_async_copy(expert_hbm, experts, sem.at[0])
    second = pltpu.make_async_copy(tokens_hbm.at[:, side_of(core, half)], mine, sem.at[1])
    first.start()
    second.start()
    first.wait()
    placing = place_rows(experts, capacity)
    second.wait()
    packed = dot(placing, mine[...], MATMUL).astype(BF16)
    for k in range(count):
        outs[k][...] = packed[k * capacity : (k + 1) * capacity]


def place_kernel(capacity, expert_ref, out):
    out[...] = jnp.transpose(place_rows(expert_ref, capacity))


def unpack_kernel(placing_ref, *refs):
    *pieces, out = refs
    rows = jnp.concatenate([p[...] for p in pieces])
    out[...] = dot(placing_ref[...], rows, MATMUL).astype(BF16)


def sum_kernel(kept_ref, *refs):
    got_ref, *outs = refs
    capacity = outs[0].shape[0]
    for k, out in enumerate(outs):
        at = pl.ds(k * capacity, capacity)
        out[...] = (kept_ref[at].astype(F32) + got_ref[at].astype(F32)).astype(BF16)


def joined(refs, columns=slice(None)):
    return jnp.concatenate([r[:, columns] for r in refs])


def activations(pieces, others, rows_ref):
    half = rows_ref.shape[1] // 2
    acts = dot(joined(pieces), rows_ref[:, :half], LAST)
    return acts + dot(joined(others), rows_ref[:, half:], LAST)


def source_of(k):
    count = lax.axis_size("exp")
    return lax.rem(lax.axis_index("exp") - k + count, count)


def own_kernel(blocks, *refs):
    n = len(blocks)
    pieces, others = refs[:n], refs[n : 2 * n]
    cotan_ref, rows_ref, d_ref, sent_ref, hidden_ref = refs[2 * n :]
    capacity, units = cotan_ref.shape[1:]
    acts = activations(pieces, others, rows_ref)
    for i, k in enumerate(blocks):
        at = slice(i * capacity, (i + 1) * capacity)
        gate, up = acts[at, :units], acts[at, units:]
        sigma, d_gate, d_up = gradients(gate, up, cotan_ref[source_of(k)])
        hidden_ref[source_of(k)] = (gate * sigma * up).astype(BF16)
        d_ref[at, :units] = d_gate
        d_ref[at, units:] = d_up
    sent_ref[...] = dot(d_ref[...], rows_ref[:, sent_ref.shape[1] :], MATMUL).astype(BF16)


def kept_kernel(d_ref, rows_ref, kept_ref):
    mine = rows_ref[:, : kept_ref.shape[1]]
    kept_ref[...] = dot(d_ref[...], mine, MATMUL).astype(BF16)


def part_kernel(plan, n, *refs):
    pieces, others = refs[:n], refs[n : 2 * n]
    near, far, rows_ref, *begun, d_ref = refs[2 * n :]
    capacity, units = near.shape[1:]
    if begun:
        half = rows_ref.shape[1] // 2
        acts = begun[0][...] + dot(joined(others), rows_ref[:, half:], LAST)
    else:
        acts = activations(pieces, others, rows_ref)
    for i, (k, group) in enumerate(plan):
        at = slice(i * capacity, (i + 1) * capacity)
        source = source_of(k)
        cotan = near[source] if group == 2 else far[0 if group == 1 else 1, source]
        _, d_gate, d_up = gradients(acts[at, :units], acts[at, units:], cotan)
        d_ref[at, :units] = d_gate
        d_ref[at, units:] = d_up


def begin_kernel(*refs):
    *pieces, rows_ref, out = refs
    out[...] = dot(joined(pieces), rows_ref[:, : rows_ref.shape[1] // 2], LAST)


def hold(ds, held):
    start = 0
    for d in ds:
        held[start : start + d.shape[0]] = d[...]
        start += d.shape[0]


def grad_kernel(n, *refs):
    pieces, others = refs[:n], refs[n : 2 * n]
    *ds, out, held = refs[2 * n :]
    hold(ds, held)
    half = out.shape[1] // 2
    for j, rows in enumerate((pieces, others)):
        out[:, j * half : (j + 1) * half] = dot(held[...], joined(rows), FIRST)


def last_grad_kernel(scale, n, *refs):
    pieces, others = refs[:n], refs[n : 2 * n]
    *ds, earlier, gate_out, up_out, staged, held, sem = refs[2 * n :]
    hold(ds, held)
    core, units, half = lax.axis_index("shard"), gate_out.shape[0], staged.shape[1] // 2
    wide, copies = half // 5, []
    for j, (rows, side) in enumerate(((pieces, core), (others, 1 - core))):
        for i, (start, stop) in enumerate(((0, 2), (2, 4), (4, 5))):
            columns = slice(start * wide, stop * wide)
            at = slice(j * half + start * wide, j * half + stop * wide)
            total = dot(held[...], joined(rows, columns), FIRST)
            staged[:, at] = ((total + earlier[:, at]) * scale).astype(BF16)
            to = pl.ds(pl.multiple_of(side * half + start * wide, 128), (stop - start) * wide)
            for h, out in enumerate((gate_out, up_out)):
                copies.append(
                    pltpu.make_async_copy(
                        staged.at[h * units : (h + 1) * units, at], out.at[:, to], sem.at[j, i, h]
                    )
                )
                copies[-1].start()
    for c in copies:
        c.wait()


def swap(x):
    return across(x, "shard", 1)


def gather_plan(tokens, expert_of, w_gate, w_up, d_hidden):
    count = lax.axis_size("exp")
    capacity = d_hidden.shape[3]
    width = tokens.shape[1]
    half = width // 2
    hidden_width = w_gate.shape[1]
    gate_rows, up_rows, cotan = w_gate[0], w_up[0], d_hidden[0, 0]
    experts = expert_of.reshape(1, -1)
    piece = like(capacity, half)

    def own(pair, rows, others):
        n = len(pair) * capacity
        return call(
            functools.partial(own_kernel, pair),
            [VMEM] * (2 * len(rows) + 2),
            [like(n, 2 * hidden_width), like(n, half), like(len(pair), capacity, hidden_width)],
            [*rows, *others, cotan, both_rows],
            name="own",
        )

    def part(plan, pieces, others, near, far, begun=()):
        n = sum(p.shape[0] for p in pieces)
        (d,) = call(
            functools.partial(part_kernel, plan, len(pieces)),
            [VMEM] * (2 * len(pieces) + 3 + len(begun)),
            [like(n, 2 * hidden_width)],
            [*pieces, *others, near, far, both_rows, *begun],
            name="part",
        )
        return d

    def add(kept, got):
        return call(sum_kernel, [VMEM] * 2, [piece] * count, [kept, got], name="sum")

    packing = [pltpu.with_memory_space_constraint(x, pltpu.HBM) for x in (experts, tokens)]
    blocks = call(
        functools.partial(pack_kernel, capacity),
        [HBM, HBM],
        [piece] * count,
        packing,
        scratch=[
            pltpu.VMEM(experts.shape, jnp.int32),
            pltpu.VMEM((tokens.shape[0], half), BF16),
            pltpu.SemaphoreType.DMA((2,)),
        ],
        name="pack",
    )
    c0 = blocks[0]
    z1, z2, z3 = (turned(blocks[k], "exp", k) for k in (1, 2, 3))
    (cotan_sent,) = after([cotan], c0)
    c0_near = across(c0, "rep", 1)
    cotan_near = across(cotan_sent, "rep", 2)
    weights = [pltpu.with_memory_space_constraint(x, pltpu.HBM) for x in (gate_rows, up_rows)]
    both_rows, other = call(
        functools.partial(load_kernel, capacity),
        [HBM] * 4,
        [like(2 * hidden_width, width), piece],
        [*after(weights, c0), *packing],
        scratch=[
            pltpu.VMEM(experts.shape, jnp.int32),
            pltpu.VMEM((tokens.shape[0], half), BF16),
            pltpu.SemaphoreType.DMA((2, 2)),
            pltpu.SemaphoreType.DMA((2,)),
        ],
        name="load",
    )
    c0_kept, c0_near_kept = after([c0, c0_near], both_rows)
    c0_both = jnp.concatenate([c0_kept, c0_near_kept])
    cotan_both = jnp.stack([cotan, cotan_near])
    c0_far = across(c0_both, "rep", 2)
    cotan_far = across(cotan_both, "rep", 1)

    z1, z2, z3 = after([z1, z2, z3], c0_both, cotan_both)
    o1, o2, o3 = swap(z1), swap(z2), swap(z3)
    c123 = jnp.concatenate([z1, z2, z3])
    o1, o2, o3 = after([o1, o2, o3], c0_far, cotan_far)
    d_a, sent, hidden = own((0, 1, 2, 3), [c0, z1, z2, z3], [other, o1, o2, o3])
    (kept,) = call(
        kept_kernel, [VMEM] * 2, [like(count * capacity, half)], [d_a, both_rows], name="kept"
    )
    c123_sent, c0_near_sent, c0_far_sent = after([c123, c0_near, c0_far], sent)
    c123_x, c123_y = across(c123_sent, "rep", 1), across(c123_sent, "rep", 2)
    c0_others = [swap(c0_near_sent), swap(c0_far_sent)]
    r0, r1, r2, r3 = add(kept, swap(sent))
    r1, r2, r3 = turned(r1, "exp", -1), turned(r2, "exp", -2), turned(r3, "exp", -3)

    plan = ((0, 1), (0, 2), (0, 3))
    d_c = part(plan, [c0_near, c0_far], c0_others, cotan_near, cotan_far)
    (total,) = call(
        functools.partial(grad_kernel, 6),
        [VMEM] * 14,
        [like(2 * hidden_width, width, dtype=F32)],
        [c0, z1, z2, z3, c0_near, c0_far, other, o1, o2, o3, *c0_others, d_a, d_c],
        scratch=[pltpu.VMEM((d_a.shape[0] + d_c.shape[0], 2 * hidden_width), BF16)],
        name="grads_near",
        limit=32,
    )
    (placing,) = call(
        functools.partial(place_kernel, capacity),
        [VMEM],
        [like(tokens.shape[0], count * capacity)],
        after([experts], d_c),
        name="place",
    )
    c123_x, c123_y = after([c123_x, c123_y], total, placing)
    cut = (c123.shape[0] // 2 + 15) // 16 * 16
    far_sent = [across(c123_x[:cut], "rep", 2), across(c123_y[cut:], "rep", 1)]
    (c123_x,), (c123_y,) = after([c123_x], r1), after([c123_y], r2)
    (begun,) = call(
        begin_kernel,
        [VMEM] * 3,
        [like(2 * c123.shape[0], 2 * hidden_width, dtype=F32)],
        [c123_x, c123_y, both_rows],
        name="begin",
    )
    (r3,) = after([r3], begun)
    (d_tokens,) = call(
        unpack_kernel,
        [VMEM] * (1 + count),
        [like(tokens.shape[0], half)],
        [placing, r0, r1, r2, r3],
        name="unpack",
        flops=6*10**9,
    )
    far_sent = after(far_sent, d_tokens)
    plan = tuple((k, group) for group in (1, 2) for k in (1, 2, 3))
    pieces, others = [c123_x, c123_y], [swap(c123_x), swap(c123_y)]
    d_d = part(plan, pieces, others, cotan_near, cotan_far, [begun])
    plan = tuple((k, 3) for k in (1, 2, 3))
    far_others = after([swap(f) for f in far_sent], d_d)
    d_e = part(plan, far_sent, far_others, cotan_near, cotan_far)
    grad_gate, grad_up = call(
        functools.partial(last_grad_kernel, 1.0 / lax.axis_size("rep"), 4),
        [VMEM] * 11,
        [like(hidden_width, width)] * 2,
        [*pieces, *far_sent, *others, *far_others, d_d, d_e, total],
        scratch=[
            pltpu.VMEM((2 * hidden_width, width), BF16),
            pltpu.VMEM((d_d.shape[0] + d_e.shape[0], 2 * hidden_width), BF16),
            pltpu.SemaphoreType.DMA((2, 3, 2)),
        ],
        name="grads",
        limit=32,
        out_spec=HBM,
    )
    return hidden.reshape(d_hidden.shape), d_tokens, grad_gate[None], grad_up[None]


def local(tokens, expert_of, w_gate, w_up, d_hidden):
    replica_count, shard_count = lax.axis_size("rep"), lax.axis_size("shard")
    slots_all = d_hidden.shape[2] * d_hidden.shape[3]
    hidden_width, feature_width = w_gate.shape[1:]
    gathered = slots_all * (feature_width // shard_count + hidden_width) * replica_count
    reduced = 4 * hidden_width * feature_width
    if replica_count == 4 and shard_count == 2 and lax.axis_size("exp") == 4 and gathered < reduced:
        return gather_plan(tokens, expert_of, w_gate, w_up, d_hidden)
    return reduce_plan(tokens, expert_of, w_gate, w_up, d_hidden)


def solution(mesh):
    in_specs = (
        P(("rep", "exp"), None),
        P(("rep", "exp"), None),
        P("exp", "shard", None),
        P("exp", "shard", None),
        P("rep", "exp", None, None, "shard"),
    )
    out_specs = (
        P("rep", "exp", None, None, "shard"),
        P(("rep", "exp"), "shard"),
        P("exp", "shard", None),
        P("exp", "shard", None),
    )
    return jax.shard_map(local, mesh=mesh, in_specs=in_specs, out_specs=out_specs, check_vma=False)
```
